512 devices in a mesh: ctx: 64 (over z, y), grp: 8 (over x, core).
Axes of the slice: x: 4, y: 4, z: 16, core: 2. Of those that a mesh axis runs over, the one named last changes fastest.
Arguments:
- query_in: bfloat16 [8192, 8192], P('ctx', 'grp'), may hold values from -6 to 6
- key_in: bfloat16 [8192, 8192], P('ctx', 'grp'), may hold values from -6 to 6
- value_in: bfloat16 [8192, 8192], P('ctx', 'grp'), may hold values from -6 to 6
- short_taps: float32 [3, 3, 8192], P(None, None, 'grp'), may hold values from -3 to 3
- decay_rate: float32 [16, 8192], P(None, 'grp'), may hold values from 0 to 1, as said below
- residues: float32 [16, 8192], P(None, 'grp'), may hold values from -2.5 to 2.5
- doc_lengths: int32 [32], replicated, may hold values from 1 to 2048, 8192 in all
- residual: bfloat16 [8192, 8192], P('ctx', 'grp'), may hold values from -6 to 6
- norm_gain: float32 [8192], P('grp'), may hold values from 0.5 to 1.5
Outputs:
- hidden_out: bfloat16 [8192, 8192], P('ctx', 'grp')
- normed: bfloat16 [8192, 8192], P('ctx', 'grp')
The draws below stay inside these ranges and needn't reach their ends.
Inputs may be any that keep to these rules, and one draw needn't show every extreme that they name: `doc_lengths`: the lengths are positive, sum to 8192, and the largest is exactly 2048. `decay_rate`: positive decay rates.
All inputs are finite; a program needn't handle non-finite values.
Results may differ from the reference program's by a relative error of at most 0.0045.
Values may be sent and summed in bfloat16 or wider, within the bound.
A program may use at most 128 MiB of HBM per device.

```python
import math
import jax
import jax.numpy as jnp
import numpy as np
from jax import lax

D = 8192
STATE = 16
KS = 3
TOKENS = 8192
NDOC = 32
MAXDOC = 2048


def draw_decay_rate(key, part):
    key_rate = jax.random.fold_in(key, 23)
    spread = jax.random.uniform(key_rate, (STATE, D), jnp.float32)
    low_end = jnp.log(jnp.float32(0.5) / MAXDOC)
    high_end = jnp.log(jnp.float32(1.0 / 40.0))
    rate_vals = jnp.exp(high_end + spread * (low_end - high_end))
    return rate_vals


def levels(key, shape, split, smallest, top_value):
    def one(dim, shards_of):
        steps = jax.random.uniform(jax.random.fold_in(jax.random.fold_in(key, 6), dim), (shards_of,), jnp.float32, smallest / len(split), top_value / len(split))
        return jnp.repeat(jnp.exp(steps), shape[dim] // shards_of).reshape((-1,) + (1,) * (len(shape) - dim - 1))

    factor_of = one(*split[0])
    for cut in split[1:]:
        factor_of = factor_of * one(*cut)
    return factor_of


def split_up(number_of, total, most, lean):
    portions = [(1 << 20) // math.isqrt(grade ** lean) + 1 for grade in range(2, number_of + 1)]
    spare, counts = total - most - (number_of - 1), [1] * (number_of - 1)
    while spare > 0:
        free = [i for i in range(number_of - 1) if counts[i] < most]
        whole, remaining = sum([portions[i] for i in free]), spare
        for i in free:
            more = min(most - counts[i], max(1, remaining * portions[i] // whole), spare)
            counts[i] = counts[i] + more
            spare = spare - more
    return np.array([most] + counts)


def uneven(own_key, number_of, total, reach, skew):
    if number_of == 2:
        one = jax.random.randint(own_key, (), max(1, total - reach), min(reach, total - 1) + 1)
        return jnp.stack([one, total - one])
    sizes = jnp.asarray(split_up(number_of, total, reach, skew), jnp.int32)
    twos = (number_of - 1) // 2
    source_of, receiver = sizes[1:1 + 2 * twos:2], sizes[2:2 + 2 * twos:2]
    room = jnp.minimum(source_of - 1, reach - receiver)
    shifted = jax.random.randint(jax.random.fold_in(own_key, 1), (twos,), 0, 1 << 20) % (room + 1)
    sizes = sizes.at[1:1 + 2 * twos:2].set(source_of - shifted).at[2:2 + 2 * twos:2].set(receiver + shifted)
    return sizes[jax.random.permutation(jax.random.fold_in(own_key, 2), number_of)]


def centred(stream_key, shape, scale, limit, split=(), kind=jnp.bfloat16):
    entries = scale * jax.random.normal(stream_key, shape, jnp.float32)
    if split:
        entries = entries * levels(stream_key, shape, split, -0.22, 0.18)
    return jnp.clip(entries, -limit, limit).astype(kind)


def setup_inputs(seed: int = 0) -> dict:
    streams_of = jax.random.split(jax.random.key(seed), 10)
    query_in = centred(streams_of[0], (TOKENS, D), 1.0, 6.0, ((0, 64), (1, 8)))
    key_in = centred(streams_of[1], (TOKENS, D), 1.0, 6.0, ((0, 64), (1, 8)))
    value_in = centred(streams_of[2], (TOKENS, D), 1.0, 6.0, ((0, 64), (1, 8)))
    short_taps = centred(streams_of[3], (3, KS, D), 0.6, 3.0, ((2, 8),), jnp.float32)
    decay_rate = draw_decay_rate(jax.random.fold_in(streams_of[9], 71), 0)
    residues = centred(streams_of[5], (STATE, D), 0.25, 2.5, ((1, 8),), jnp.float32)
    doc_lengths = uneven(streams_of[6], NDOC, TOKENS, MAXDOC, 2).astype(jnp.int32)
    residual = centred(streams_of[7], (TOKENS, D), 1.0, 6.0, ((0, 64), (1, 8)))
    norm_gain = jnp.clip(1.0 + 0.1 * jax.random.normal(streams_of[8], (D,), jnp.float32), 0.5, 1.5)
    return dict(query_in=query_in, key_in=key_in, value_in=value_in, short_taps=short_taps, decay_rate=decay_rate, residues=residues, doc_lengths=doc_lengths, residual=residual, norm_gain=norm_gain)


def short_conv(signal, taps, keep_one, keep_two):
    padded = jnp.pad(signal, ((2, 0), (0, 0)))
    return taps[0] * signal + taps[1] * padded[1:-1] * keep_one[:, None] + taps[2] * padded[:-2] * keep_two[:, None]

def segment_conv(gate_val, rate_blk, weight_blk, fresh_flags):
    decay_step = jnp.exp(-rate_blk)

    def advance(carried, inputs):
        gate_row, restart = inputs
        carried = decay_step * carried * (1.0 - restart) + gate_row[None, :]
        return (carried, lax.optimization_barrier(jnp.sum(weight_blk * carried, axis=0)))
    _, conv_full = lax.scan(advance, jnp.zeros(rate_blk.shape, jnp.float32), (gate_val, fresh_flags))
    return conv_full

def reference(query_in, key_in, value_in, short_taps, decay_rate, residues, doc_lengths, residual, norm_gain):
    lengths = doc_lengths.astype(jnp.int32)
    starts = (jnp.cumsum(lengths) - lengths).astype(jnp.int32)
    positions = jnp.arange(TOKENS, dtype=jnp.int32)
    flag_here = jnp.any(positions[:, None] == starts[None, :], axis=1)
    flag_prev = jnp.any((positions - 1)[:, None] == starts[None, :], axis=1)
    keep_one = jnp.logical_not(flag_here).astype(jnp.float32)
    keep_two = jnp.logical_not(jnp.logical_or(flag_here, flag_prev)).astype(jnp.float32)
    fresh_flags = flag_here.astype(jnp.float32)
    weight = residues * jnp.sqrt(-jnp.expm1(-2.0 * decay_rate))
    blocks = D // 512

    def split_cols(array):
        return array.reshape(TOKENS, blocks, 512).transpose(1, 0, 2)

    def split_modes(array):
        return array.reshape(STATE, blocks, 512).transpose(1, 0, 2)
    taps_blocks = short_taps.reshape(3, KS, blocks, 512).transpose(2, 0, 1, 3)

    def branch_block(packed):
        query_blk, key_blk, value_blk, taps_blk, rate_blk, weight_blk = packed
        q_short = short_conv(query_blk.astype(jnp.float32), taps_blk[0], keep_one, keep_two)
        k_short = short_conv(key_blk.astype(jnp.float32), taps_blk[1], keep_one, keep_two)
        v_short = short_conv(value_blk.astype(jnp.float32), taps_blk[2], keep_one, keep_two)
        gate_in = lax.optimization_barrier((k_short * v_short).astype(jnp.bfloat16))
        conv_full = segment_conv(gate_in.astype(jnp.float32), rate_blk, weight_blk, fresh_flags)
        conv_out = lax.optimization_barrier(conv_full.astype(jnp.bfloat16))
        return q_short * conv_out.astype(jnp.float32)
    branch = lax.map(branch_block, (split_cols(query_in), split_cols(key_in), split_cols(value_in), taps_blocks, split_modes(decay_rate), split_modes(weight)))
    branch = branch.transpose(1, 0, 2).reshape(TOKENS, D)
    hidden = residual.astype(jnp.float32) + branch
    hidden_out = hidden.astype(jnp.bfloat16)
    inverse_rms = lax.rsqrt(lax.optimization_barrier(jnp.mean(hidden * hidden, axis=1, keepdims=True)) + 1e-06)
    normed = (hidden * inverse_rms * norm_gain[None, :]).astype(jnp.bfloat16)
    return (hidden_out, normed)
```

```python
import functools

import jax
import jax.numpy as jnp
from jax import lax
from jax.experimental import pallas as pl
from jax.experimental.pallas import tpu as pltpu
from jax.sharding import PartitionSpec as P

D = 8192
MESH = pl.DeviceIdType.MESH
F32 = jnp.float32
BF16 = jnp.bfloat16
YN = 4
BACK = 4


def decay_weight(rate, residue):
    x = 2.0 * rate
    series = 1.0 - x / 8.0
    for k in (7.0, 6.0, 5.0, 4.0, 3.0, 2.0):
        series = 1.0 - (x / k) * series
    one_minus = jnp.where(x < 0.25, x * series, 1.0 - jnp.exp(-x))
    return residue * jnp.sqrt(one_minus)


def block_kernel(
    nctx,
    ngrp,
    doc_ref,
    q_ref,
    k_ref,
    v_ref,
    taps_ref,
    rate_ref,
    res_ref,
    resid_ref,
    gain_ref,
    hid_ref,
    norm_ref,
    tail_ref,
    halo_ref,
    qs_ref,
    g_ref,
    y_ref,
    keep_ref,
    pre_ref,
    carry_ref,
    nat_ref,
    a_ref,
    w_ref,
    rate3_ref,
    e_ref,
    r1_ref,
    t_ref,
    r2_ref,
    i_ref,
    r3_ref,
    ss_ref,
    rs_ref,
    halo_send,
    halo_recv,
    s1,
    v1,
    s2,
    v2,
    s3,
    v3,
    s4,
    v4,
):
    tok, chans = q_ref.shape
    lanes = 128
    tiles = chans // lanes
    modes = rate_ref.shape[0]
    ndoc = doc_ref.shape[0]
    quarter = modes // YN
    zn = nctx // YN
    me = lax.axis_index("ctx")
    gi = lax.axis_index("grp")
    z = me // YN
    yy = lax.rem(me, YN)

    def in_plane(k):
        return z * YN + lax.rem(yy + k, YN)

    def plane(k):
        return lax.rem(z + k + zn, zn) * YN + yy

    barrier = pltpu.get_barrier_semaphore()
    pl.semaphore_signal(
        barrier, inc=1, device_id={"ctx": lax.rem(me + nctx - 1, nctx)}, device_id_type=MESH
    )
    for k in range(1, YN):
        pl.semaphore_signal(
            barrier, inc=1, device_id={"ctx": in_plane(YN - k)}, device_id_type=MESH
        )
    for k in range(1, BACK + 1):
        pl.semaphore_signal(barrier, inc=1, device_id={"ctx": plane(-k)}, device_id_type=MESH)
    for k in range(1, ngrp):
        pl.semaphore_signal(
            barrier, inc=1, device_id={"grp": lax.rem(gi + ngrp - k, ngrp)}, device_id_type=MESH
        )

    for i, ref in enumerate((q_ref, k_ref, v_ref)):
        tail_ref[2 * i : 2 * i + 2, :] = ref[tok - 16 :, :].astype(F32)[14:16]
    tail_ref[6:8, :] = jnp.zeros((2, chans), F32)

    rate = rate_ref[...]
    for slot, value, dest in (
        (0, jnp.exp(-rate), a_ref),
        (1, decay_weight(rate, res_ref[...]), w_ref),
        (2, rate, rate3_ref),
    ):
        for j in range(tiles):
            nat_ref[slot, j * modes : (j + 1) * modes, :] = value[:, j * lanes : (j + 1) * lanes]
        for n in range(modes):
            dest[n] = nat_ref[slot, pl.ds(n, tiles, stride=modes), :]

    row = lax.broadcasted_iota(jnp.int32, (tok, lanes), 0)
    brow = lax.broadcasted_iota(jnp.int32, (nctx, lanes), 0)
    p0 = me * tok
    start = jnp.int32(0)
    first = jnp.int32(tok)
    before = jnp.int32(0)
    fresh = jnp.zeros((tok, lanes), F32)
    opens = jnp.zeros((nctx, lanes), F32)
    for d in range(ndoc):
        rel = start - p0
        fresh = jnp.where(row == rel, 1.0, fresh)
        opens = jnp.where(brow == start // tok, 1.0, opens)
        before = jnp.where(rel == -1, 1, before)
        first = jnp.where(rel >= 0, jnp.minimum(first, rel), first)
        start = start + doc_ref[d]
    keep_one = 1.0 - fresh
    keep_ref[...] = keep_one
    pre_ref[...] = jnp.where(row < first, 1.0, 0.0)
    carry_ref[...] = 1.0 - opens
    keep_prev = jnp.where(row == 0, (1 - before).astype(F32), pltpu.roll(keep_one, 1, 0))
    keep_two = keep_one * keep_prev

    pl.semaphore_wait(barrier, 1 + (YN - 1) + BACK + (ngrp - 1))

    halo = pltpu.make_async_remote_copy(
        src_ref=tail_ref,
        dst_ref=halo_ref,
        send_sem=halo_send,
        recv_sem=halo_recv,
        device_id={"ctx": lax.rem(me + 1, nctx)},
        device_id_type=MESH,
    )
    halo.start()
    halo.wait()

    def short(ref, i, j):
        cols = slice(j * lanes, (j + 1) * lanes)
        x = ref[:, cols].astype(F32)
        h0 = halo_ref[2 * i : 2 * i + 1, cols]
        h1 = halo_ref[2 * i + 1 : 2 * i + 2, cols]
        one = jnp.where(row == 0, h1, pltpu.roll(x, 1, 0)) * keep_one
        two = jnp.where(row == 0, h0, jnp.where(row == 1, h1, pltpu.roll(x, 2, 0))) * keep_two
        return (
            taps_ref[i, 0:1, cols] * x + taps_ref[i, 1:2, cols] * one + taps_ref[i, 2:3, cols] * two
        )

    for j in range(tiles):
        gate = short(k_ref, 1, j) * short(v_ref, 2, j)
        g_ref[j * tok : (j + 1) * tok, :] = gate.astype(BF16).astype(F32)

    def scan_step(t, states):
        g = g_ref[pl.ds(t, tiles, stride=tok), :]
        keep = keep_ref[pl.ds(t, 1), :]
        new = []
        total = None
        for n in range(modes):
            s = (a_ref[n] * keep) * states[n] + g
            term = w_ref[n] * s
            total = term if total is None else total + term
            new.append(s)
        y_ref[pl.ds(t, tiles, stride=tok), :] = total
        return tuple(new)

    zero = jnp.zeros((tiles, lanes), F32)
    states = lax.fori_loop(0, tok, scan_step, (zero,) * modes, unroll=4)
    for n in range(modes):
        e_ref[n] = states[n]

    sends = []
    for k in range(1, YN):
        to = lax.rem(yy + k, YN)
        sends.append(
            pltpu.make_async_remote_copy(
                src_ref=e_ref.at[pl.ds(to * quarter, quarter)],
                dst_ref=r1_ref.at[k],
                send_sem=s1.at[k],
                recv_sem=v1.at[k],
                device_id={"ctx": in_plane(k)},
                device_id_type=MESH,
            )
        )
    for copy in sends:
        copy.start()
    r1_ref[0] = e_ref[pl.ds(yy * quarter, quarter)]
    for j in range(tiles):
        qs_ref[j * tok : (j + 1) * tok, :] = short(q_ref, 0, j)
    rate_q = rate3_ref[pl.ds(yy * quarter, quarter)]
    decay_blk = jnp.exp(-float(tok) * rate_q)
    decay_plane = jnp.exp(-float(tok * YN) * rate_q)

    def carry_of(block):
        return carry_ref[pl.ds(block, 1), :][None]

    def plane_carry(k):
        base = lax.rem(z - k + zn, zn) * YN
        value = carry_of(base)
        for j in range(1, YN):
            value = value * carry_of(base + j)
        return value

    for copy in sends:
        copy.wait()

    ends = [r1_ref[lax.rem(yy - j + YN, YN)] for j in range(YN)]
    total = ends[0]
    for j in range(1, YN):
        total = ends[j] + decay_blk * carry_of(z * YN + j) * total
    t_ref[...] = total

    sends = []
    for k in range(1, BACK + 1):
        sends.append(
            pltpu.make_async_remote_copy(
                src_ref=t_ref,
                dst_ref=r2_ref.at[k - 1],
                send_sem=s2.at[k - 1],
                recv_sem=v2.at[k - 1],
                device_id={"ctx": plane(k)},
                device_id_type=MESH,
            )
        )
    for copy in sends:
        copy.start()
    for copy in sends:
        copy.wait()
    enter = r2_ref[BACK - 1]
    for k in range(BACK - 1, 0, -1):
        enter = r2_ref[k - 1] + decay_plane * plane_carry(k) * enter
    for j in range(YN):
        i_ref[j] = enter
        if j < YN - 1:
            enter = ends[j] + decay_blk * carry_of(z * YN + j) * enter

    sends = []
    for k in range(1, YN):
        to = lax.rem(yy + k, YN)
        sends.append(
            pltpu.make_async_remote_copy(
                src_ref=i_ref.at[to],
                dst_ref=r3_ref.at[k],
                send_sem=s3.at[k],
                recv_sem=v3.at[k],
                device_id={"ctx": in_plane(k)},
                device_id_type=MESH,
            )
        )
    for copy in sends:
        copy.start()
    r3_ref[0] = i_ref[yy]
    for copy in sends:
        copy.wait()

    entering = []
    for m in range(YN):
        part = r3_ref[lax.rem(yy - m + YN, YN)]
        for n in range(quarter):
            entering.append(w_ref[m * quarter + n] * part[n])

    def fix_step(t, states):
        new = []
        total = None
        for n in range(modes):
            s = a_ref[n] * states[n]
            total = s if total is None else total + s
            new.append(s)
        at = pl.ds(t, tiles, stride=tok)
        y_ref[at, :] = y_ref[at, :] + pre_ref[pl.ds(t, 1), :] * total
        return tuple(new)

    lax.fori_loop(0, tok, fix_step, tuple(entering), unroll=4)

    squares = jnp.zeros((tok, lanes), F32)
    for j in range(tiles):
        rows = slice(j * tok, (j + 1) * tok)
        cols = slice(j * lanes, (j + 1) * lanes)
        conv = y_ref[rows, :].astype(BF16).astype(F32)
        hidden = resid_ref[:, cols].astype(F32) + qs_ref[rows, :] * conv
        squares = squares + hidden * hidden
        qs_ref[rows, :] = hidden
        hid_ref[:, cols] = hidden.astype(BF16)
    by_token = jnp.sum(squares.T, axis=0, keepdims=True)
    ss_ref[...] = jnp.broadcast_to(by_token, (8, lanes))
    sends = []
    for k in range(1, ngrp):
        sends.append(
            pltpu.make_async_remote_copy(
                src_ref=ss_ref,
                dst_ref=rs_ref.at[k],
                send_sem=s4.at[k],
                recv_sem=v4.at[k],
                device_id={"grp": lax.rem(gi + k, ngrp)},
                device_id_type=MESH,
            )
        )
    for copy in sends:
        copy.start()
    for copy in sends:
        copy.wait()
    total = ss_ref[...]
    for k in range(1, ngrp):
        total = total + rs_ref[k]
    inverse = lax.rsqrt(total * (1.0 / D) + 1e-06)
    inverse = jnp.broadcast_to(inverse[0:1, :], (lanes, tok)).T
    for j in range(tiles):
        rows = slice(j * tok, (j + 1) * tok)
        cols = slice(j * lanes, (j + 1) * lanes)
        norm_ref[:, cols] = (qs_ref[rows, :] * inverse * gain_ref[:, cols]).astype(BF16)


def shards(
    nctx,
    ngrp,
    query_in,
    key_in,
    value_in,
    short_taps,
    decay_rate,
    residues,
    doc_lengths,
    residual,
    norm_gain,
):
    tok, chans = query_in.shape
    modes = decay_rate.shape[0]
    tiles = chans // 128
    quarter = modes // YN
    vmem = pl.BlockSpec(memory_space=pltpu.VMEM)
    state = (modes, tiles, 128)
    part = (quarter, tiles, 128)
    dma = pltpu.SemaphoreType.DMA
    return pl.pallas_call(
        functools.partial(block_kernel, nctx, ngrp),
        out_shape=(
            jax.ShapeDtypeStruct((tok, chans), BF16),
            jax.ShapeDtypeStruct((tok, chans), BF16),
        ),
        in_specs=[pl.BlockSpec(memory_space=pltpu.SMEM)] + [vmem] * 8,
        out_specs=(vmem, vmem),
        scratch_shapes=[
            pltpu.VMEM((8, chans), F32),
            pltpu.VMEM((8, chans), F32),
            pltpu.VMEM((tiles * tok, 128), F32),
            pltpu.VMEM((tiles * tok, 128), F32),
            pltpu.VMEM((tiles * tok, 128), F32),
            pltpu.VMEM((tok, 128), F32),
            pltpu.VMEM((tok, 128), F32),
            pltpu.VMEM((nctx, 128), F32),
            pltpu.VMEM((3, tiles * modes, 128), F32),
            pltpu.VMEM(state, F32),
            pltpu.VMEM(state, F32),
            pltpu.VMEM(state, F32),
            pltpu.VMEM(state, F32),
            pltpu.VMEM((YN,) + part, F32),
            pltpu.VMEM(part, F32),
            pltpu.VMEM((BACK,) + part, F32),
            pltpu.VMEM((YN,) + part, F32),
            pltpu.VMEM((YN,) + part, F32),
            pltpu.VMEM((8, 128), F32),
            pltpu.VMEM((ngrp, 8, 128), F32),
            dma,
            dma,
            dma((YN,)),
            dma((YN,)),
            dma((BACK,)),
            dma((BACK,)),
            dma((YN,)),
            dma((YN,)),
            dma((ngrp,)),
            dma((ngrp,)),
        ],
        compiler_params=pltpu.CompilerParams(collective_id=0, has_side_effects=True),
        name="hyena_block",
    )(
        doc_lengths,
        query_in,
        key_in,
        value_in,
        short_taps,
        decay_rate,
        residues,
        residual,
        norm_gain.reshape(1, chans),
    )


def solution(mesh):
    return jax.shard_map(
        functools.partial(shards, mesh.shape["ctx"], mesh.shape["grp"]),
        mesh=mesh,
        in_specs=(
            P("ctx", "grp"),
            P("ctx", "grp"),
            P("ctx", "grp"),
            P(None, None, "grp"),
            P(None, "grp"),
            P(None, "grp"),
            P(),
            P("ctx", "grp"),
            P("grp"),
        ),
        out_specs=(P("ctx", "grp"), P("ctx", "grp")),
        check_vma=False,
    )
```

```python
import functools

import jax
import jax.numpy as jnp
from jax import lax
from jax.experimental import pallas as pl
from jax.experimental.pallas import tpu as pltpu
from jax.sharding import PartitionSpec as P

D = 8192
MESH = pl.DeviceIdType.MESH
F32 = jnp.float32
BF16 = jnp.bfloat16
YN = 4
BACK = 4


def decay_weight(rate, residue):
    x = 2.0 * rate
    series = 1.0 - x / 8.0
    for k in (7.0, 6.0, 5.0, 4.0, 3.0, 2.0):
        series = 1.0 - (x / k) * series
    one_minus = jnp.where(x < 0.25, x * series, 1.0 - jnp.exp(-x))
    return residue * jnp.sqrt(one_minus)


def block_kernel(
    nctx,
    ngrp,
    doc_hbm,
    q_hbm,
    k_hbm,
    v_hbm,
    taps_hbm,
    rate_hbm,
    res_hbm,
    resid_hbm,
    gain_hbm,
    hid_hbm,
    norm_hbm,
    doc_ref,
    q_ref,
    k_ref,
    v_ref,
    taps_ref,
    rate_ref,
    res_ref,
    resid_ref,
    gain_ref,
    hid_ref,
    norm_ref,
    tail_ref,
    halo_ref,
    qs_ref,
    g_ref,
    y_ref,
    keep_ref,
    pre_ref,
    late_ref,
    carry_ref,
    nat_ref,
    a_ref,
    w_ref,
    rate3_ref,
    e_ref,
    r1_ref,
    t_ref,
    r2_ref,
    i_ref,
    r3_ref,
    ss_ref,
    rs_ref,
    load_sem,
    store_sem,
    halo_send,
    halo_recv,
    s1,
    v1,
    s2,
    v2,
    s3,
    v3,
    s4,
    v4,
):
    tok, chans = q_ref.shape
    lanes = 128
    sub = 8
    chunks = tok // sub
    tiles = chans // lanes
    modes = rate_ref.shape[0]
    ndoc = doc_ref.shape[0]
    quarter = modes // YN
    zn = nctx // YN
    me = lax.axis_index("ctx")
    gi = lax.axis_index("grp")
    z = me // YN
    yy = lax.rem(me, YN)

    def in_plane(k):
        return z * YN + lax.rem(yy + k, YN)

    def plane(k):
        return lax.rem(z + k + zn, zn) * YN + yy

    barrier = pltpu.get_barrier_semaphore()
    pl.semaphore_signal(
        barrier, inc=1, device_id={"ctx": lax.rem(me + nctx - 1, nctx)}, device_id_type=MESH
    )
    for k in range(1, YN):
        pl.semaphore_signal(
            barrier, inc=1, device_id={"ctx": in_plane(YN - k)}, device_id_type=MESH
        )
    for k in range(1, BACK + 1):
        pl.semaphore_signal(barrier, inc=1, device_id={"ctx": plane(-k)}, device_id_type=MESH)
    for k in range(1, ngrp):
        pl.semaphore_signal(
            barrier, inc=1, device_id={"grp": lax.rem(gi + ngrp - k, ngrp)}, device_id_type=MESH
        )

    pairs = (
        (doc_hbm, doc_ref),
        (k_hbm, k_ref),
        (v_hbm, v_ref),
        (q_hbm, q_ref),
        (rate_hbm, rate_ref),
        (taps_hbm, taps_ref),
        (res_hbm, res_ref),
        (resid_hbm, resid_ref),
        (gain_hbm, gain_ref),
    )
    loads = [
        pltpu.make_async_copy(src, dst, load_sem.at[i]) for i, (src, dst) in enumerate(pairs)
    ]
    for copy in loads:
        copy.start()

    loads[0].wait()
    row = lax.broadcasted_iota(jnp.int32, (tok, lanes), 0)
    p0 = me * tok
    start = jnp.int32(0)
    first = jnp.int32(tok)
    last = jnp.int32(-1)
    before = jnp.int32(0)
    fresh = jnp.zeros((tok, lanes), F32)
    for d in range(ndoc):
        rel = start - p0
        fresh = jnp.where(row == rel, 1.0, fresh)
        before = jnp.where(rel == -1, 1, before)
        first = jnp.where(rel >= 0, jnp.minimum(first, rel), first)
        last = jnp.where((rel >= 0) & (rel < tok), rel, last)
        start = start + doc_ref[d]
    keep_one = 1.0 - fresh
    keep_ref[...] = keep_one
    keep_prev = jnp.where(row == 0, (1 - before).astype(F32), pltpu.roll(keep_one, 1, 0))
    keep_two = keep_one * keep_prev
    pre_ref[...] = jnp.where(row < first, 1.0, 0.0)
    late_ref[...] = jnp.where(row >= last, 1.0, 0.0)

    for copy in loads[1:4]:
        copy.wait()
    for i, ref in enumerate((q_ref, k_ref, v_ref)):
        tail_ref[2 * i : 2 * i + 2, :] = ref[tok - 16 :, :].astype(F32)[14:16]
    tail_ref[6:8, :] = jnp.zeros((2, chans), F32)
    for copy in loads[4:]:
        copy.wait()

    pl.semaphore_wait(barrier, 1 + (YN - 1) + BACK + (ngrp - 1))
    halo = pltpu.make_async_remote_copy(
        src_ref=tail_ref,
        dst_ref=halo_ref,
        send_sem=halo_send,
        recv_sem=halo_recv,
        device_id={"ctx": lax.rem(me + 1, nctx)},
        device_id_type=MESH,
    )
    halo.start()

    def by_mode(slot, value, dest):
        for j in range(tiles):
            nat_ref[slot, j * modes : (j + 1) * modes, :] = value[:, j * lanes : (j + 1) * lanes]
        for n in range(modes):
            dest[n] = nat_ref[slot, pl.ds(n, tiles, stride=modes), :]

    rate = rate_ref[...]
    by_mode(0, jnp.exp(-rate), a_ref)
    by_mode(2, rate, rate3_ref)

    def short(ref, i, j, rows, rim):
        cols = slice(j * lanes, (j + 1) * lanes)
        x = (ref[:, cols] if rows == tok else ref[0:16, cols]).astype(F32)[0:rows]
        one = pltpu.roll(x, 1, 0)
        two = pltpu.roll(x, 2, 0)
        if rim:
            at = row[0:rows]
            h0 = halo_ref[2 * i : 2 * i + 1, cols]
            h1 = halo_ref[2 * i + 1 : 2 * i + 2, cols]
            one = jnp.where(at == 0, h1, one)
            two = jnp.where(at == 0, h0, jnp.where(at == 1, h1, two))
        return (
            taps_ref[i, 0:1, cols] * x
            + taps_ref[i, 1:2, cols] * (one * keep_one[0:rows])
            + taps_ref[i, 2:3, cols] * (two * keep_two[0:rows])
        )

    for j in range(tiles):
        gate = short(k_ref, 1, j, tok, False) * short(v_ref, 2, j, tok, False)
        gate = gate.astype(BF16).astype(F32).reshape(chunks, sub, lanes)
        g_ref[:, j * sub : (j + 1) * sub, :] = gate

    def gate_at(c, r):
        return g_ref[c, pl.ds(r, tiles, stride=sub), :]

    def late_gate(c, r):
        return gate_at(c, r) * late_ref[pl.ds(c * sub + r, 1), :]

    def end_chunk(c, states, first_row=0):
        for r in range(first_row, sub):
            g = late_gate(c, r)
            states = tuple(a_ref[n] * states[n] + g for n in range(modes))
        return states

    zero = jnp.zeros((tiles, lanes), F32)
    states = end_chunk(0, (zero,) * modes, 2)
    states = lax.fori_loop(1, chunks, end_chunk, states)
    for n in range(modes):
        e_ref[n] = states[n]

    halo.wait()
    for j in range(tiles):
        gate = short(k_ref, 1, j, sub, True) * short(v_ref, 2, j, sub, True)
        g_ref[0, j * sub : (j + 1) * sub, :] = gate.astype(BF16).astype(F32)
    g0 = late_gate(0, 0)
    g1 = late_gate(0, 1)
    for n in range(modes):
        e_ref[n] = e_ref[n] + jnp.exp(-float(tok - 2) * rate3_ref[n]) * (g1 + a_ref[n] * g0)

    sends = []
    for k in range(1, YN):
        to = lax.rem(yy + k, YN)
        sends.append(
            pltpu.make_async_remote_copy(
                src_ref=e_ref.at[pl.ds(to * quarter, quarter)],
                dst_ref=r1_ref.at[k],
                send_sem=s1.at[k],
                recv_sem=v1.at[k],
                device_id={"ctx": in_plane(k)},
                device_id_type=MESH,
            )
        )
    for copy in sends:
        copy.start()
    r1_ref[0] = e_ref[pl.ds(yy * quarter, quarter)]
    by_mode(1, decay_weight(rate, res_ref[...]), w_ref)
    brow = lax.broadcasted_iota(jnp.int32, (nctx, lanes), 0)
    opens = jnp.zeros((nctx, lanes), F32)
    start = jnp.int32(0)
    for d in range(ndoc):
        opens = jnp.where(brow == start // tok, 1.0, opens)
        start = start + doc_ref[d]
    carry_ref[...] = 1.0 - opens
    rate_q = rate3_ref[pl.ds(yy * quarter, quarter)]
    decay_blk = jnp.exp(-float(tok) * rate_q)
    decay_plane = jnp.exp(-float(tok * YN) * rate_q)

    def carry_of(block):
        return carry_ref[pl.ds(block, 1), :][None]

    def plane_carry(k):
        base = lax.rem(z - k + zn, zn) * YN
        value = carry_of(base)
        for j in range(1, YN):
            value = value * carry_of(base + j)
        return value

    def scan_chunk(c, states):
        for r in range(sub):
            g = gate_at(c, r)
            keep = keep_ref[pl.ds(c * sub + r, 1), :]
            new = []
            total = None
            for n in range(modes):
                s = a_ref[n] * (keep * states[n]) + g
                term = w_ref[n] * s
                total = term if total is None else total + term
                new.append(s)
            y_ref[c, pl.ds(r, tiles, stride=sub), :] = total
            states = tuple(new)
        return states

    states = lax.fori_loop(0, chunks // 4, scan_chunk, (zero,) * modes)

    for copy in sends:
        copy.wait()

    ends = [r1_ref[lax.rem(yy - j + YN, YN)] for j in range(YN)]
    total = ends[0]
    for j in range(1, YN):
        total = ends[j] + decay_blk * carry_of(z * YN + j) * total
    t_ref[...] = total

    sends = []
    for k in range(1, BACK + 1):
        sends.append(
            pltpu.make_async_remote_copy(
                src_ref=t_ref,
                dst_ref=r2_ref.at[k - 1],
                send_sem=s2.at[k - 1],
                recv_sem=v2.at[k - 1],
                device_id={"ctx": plane(k)},
                device_id_type=MESH,
            )
        )
    for copy in reversed(sends):
        copy.start()
    lax.fori_loop(chunks // 4, chunks, scan_chunk, states)
    for j in range(tiles):
        cols = slice(j * lanes, (j + 1) * lanes)
        qs_ref[:, cols] = short(q_ref, 0, j, tok, True)
    for copy in sends:
        copy.wait()
    enter = r2_ref[BACK - 1]
    for k in range(BACK - 1, 0, -1):
        enter = r2_ref[k - 1] + decay_plane * plane_carry(k) * enter
    for j in range(YN):
        i_ref[j] = enter
        if j < YN - 1:
            enter = ends[j] + decay_blk * carry_of(z * YN + j) * enter

    sends = []
    for k in range(1, YN):
        to = lax.rem(yy + k, YN)
        sends.append(
            pltpu.make_async_remote_copy(
                src_ref=i_ref.at[to],
                dst_ref=r3_ref.at[k],
                send_sem=s3.at[k],
                recv_sem=v3.at[k],
                device_id={"ctx": in_plane(k)},
                device_id_type=MESH,
            )
        )
    for copy in sends:
        copy.start()
    r3_ref[0] = i_ref[yy]
    for copy in sends:
        copy.wait()

    entering = []
    for m in range(YN):
        part = r3_ref[lax.rem(yy - m + YN, YN)]
        for n in range(quarter):
            entering.append(w_ref[m * quarter + n] * part[n])

    def fix_chunk(c, states):
        for r in range(sub):
            states = tuple(a_ref[n] * states[n] for n in range(modes))
            total = states[0]
            for n in range(1, modes):
                total = total + states[n]
            at = pl.ds(r, tiles, stride=sub)
            y_ref[c, at, :] = y_ref[c, at, :] + pre_ref[pl.ds(c * sub + r, 1), :] * total
        return states

    lax.fori_loop(0, chunks, fix_chunk, tuple(entering))

    squares = jnp.zeros((tok, lanes), F32)
    for j in range(tiles):
        cols = slice(j * lanes, (j + 1) * lanes)
        conv = y_ref[:, j * sub : (j + 1) * sub, :].reshape(tok, lanes)
        conv = conv.astype(BF16).astype(F32)
        hidden = resid_ref[:, cols].astype(F32) + qs_ref[:, cols] * conv
        squares = squares + hidden * hidden
        qs_ref[:, cols] = hidden
    by_token = jnp.sum(squares.T, axis=0, keepdims=True)
    ss_ref[...] = jnp.broadcast_to(by_token, (8, lanes))
    sends = []
    for k in range(1, ngrp):
        sends.append(
            pltpu.make_async_remote_copy(
                src_ref=ss_ref,
                dst_ref=rs_ref.at[k],
                send_sem=s4.at[k],
                recv_sem=v4.at[k],
                device_id={"grp": lax.rem(gi + k, ngrp)},
                device_id_type=MESH,
            )
        )
    for copy in sends:
        copy.start()
    hid_ref[...] = qs_ref[...].astype(BF16)
    hid_out = pltpu.make_async_copy(hid_ref, hid_hbm, store_sem.at[0])
    hid_out.start()
    for copy in sends:
        copy.wait()
    total = ss_ref[...]
    for k in range(1, ngrp):
        total = total + rs_ref[k]
    inverse = lax.rsqrt(total * (1.0 / D) + 1e-06)
    inverse = jnp.broadcast_to(inverse[0:1, :], (lanes, tok)).T
    for j in range(tiles):
        cols = slice(j * lanes, (j + 1) * lanes)
        norm_ref[:, cols] = (qs_ref[:, cols] * inverse * gain_ref[:, cols]).astype(BF16)
    norm_out = pltpu.make_async_copy(norm_ref, norm_hbm, store_sem.at[1])
    norm_out.start()
    hid_out.wait()
    norm_out.wait()


def shards(
    nctx,
    ngrp,
    query_in,
    key_in,
    value_in,
    short_taps,
    decay_rate,
    residues,
    doc_lengths,
    residual,
    norm_gain,
):
    tok, chans = query_in.shape
    modes = decay_rate.shape[0]
    tiles = chans // 128
    quarter = modes // YN
    anywhere = pl.BlockSpec(memory_space=pl.ANY)
    state = (modes, tiles, 128)
    part = (quarter, tiles, 128)
    chunked = (tok // 8, tiles * 8, 128)
    dma = pltpu.SemaphoreType.DMA
    return pl.pallas_call(
        functools.partial(block_kernel, nctx, ngrp),
        out_shape=(
            jax.ShapeDtypeStruct((tok, chans), BF16),
            jax.ShapeDtypeStruct((tok, chans), BF16),
        ),
        in_specs=[anywhere] * 9,
        out_specs=(anywhere, anywhere),
        scratch_shapes=[
            pltpu.SMEM(doc_lengths.shape, jnp.int32),
            pltpu.VMEM((tok, chans), BF16),
            pltpu.VMEM((tok, chans), BF16),
            pltpu.VMEM((tok, chans), BF16),
            pltpu.VMEM(short_taps.shape, F32),
            pltpu.VMEM(decay_rate.shape, F32),
            pltpu.VMEM(residues.shape, F32),
            pltpu.VMEM((tok, chans), BF16),
            pltpu.VMEM((1, chans), F32),
            pltpu.VMEM((tok, chans), BF16),
            pltpu.VMEM((tok, chans), BF16),
            pltpu.VMEM((8, chans), F32),
            pltpu.VMEM((8, chans), F32),
            pltpu.VMEM((tok, chans), F32),
            pltpu.VMEM(chunked, F32),
            pltpu.VMEM(chunked, F32),
            pltpu.VMEM((tok, 128), F32),
            pltpu.VMEM((tok, 128), F32),
            pltpu.VMEM((tok, 128), F32),
            pltpu.VMEM((nctx, 128), F32),
            pltpu.VMEM((3, tiles * modes, 128), F32),
            pltpu.VMEM(state, F32),
            pltpu.VMEM(state, F32),
            pltpu.VMEM(state, F32),
            pltpu.VMEM(state, F32),
            pltpu.VMEM((YN,) + part, F32),
            pltpu.VMEM(part, F32),
            pltpu.VMEM((BACK,) + part, F32),
            pltpu.VMEM((YN,) + part, F32),
            pltpu.VMEM((YN,) + part, F32),
            pltpu.VMEM((8, 128), F32),
            pltpu.VMEM((ngrp, 8, 128), F32),
            dma((9,)),
            dma((2,)),
            dma,
            dma,
            dma((YN,)),
            dma((YN,)),
            dma((BACK,)),
            dma((BACK,)),
            dma((YN,)),
            dma((YN,)),
            dma((ngrp,)),
            dma((ngrp,)),
        ],
        compiler_params=pltpu.CompilerParams(collective_id=0, has_side_effects=True),
        name="hyena_block",
    )(
        doc_lengths,
        query_in,
        key_in,
        value_in,
        short_taps,
        decay_rate,
        residues,
        residual,
        norm_gain.reshape(1, chans),
    )


def solution(mesh):
    return jax.shard_map(
        functools.partial(shards, mesh.shape["ctx"], mesh.shape["grp"]),
        mesh=mesh,
        in_specs=(
            P("ctx", "grp"),
            P("ctx", "grp"),
            P("ctx", "grp"),
            P(None, None, "grp"),
            P(None, "grp"),
            P(None, "grp"),
            P(),
            P("ctx", "grp"),
            P("grp"),
        ),
        out_specs=(P("ctx", "grp"), P("ctx", "grp")),
        check_vma=False,
    )
```

```python
import functools

import jax
import jax.numpy as jnp
from jax import lax
from jax.experimental import pallas as pl
from jax.experimental.pallas import tpu as pltpu
from jax.sharding import PartitionSpec as P

D = 8192
MESH = pl.DeviceIdType.MESH
F32 = jnp.float32
BF16 = jnp.bfloat16
YN = 4
BACK = 4


def decay_weight(rate, residue):
    x = 2.0 * rate
    series = 1.0 - x / 8.0
    for k in (7.0, 6.0, 5.0, 4.0, 3.0, 2.0):
        series = 1.0 - (x / k) * series
    one_minus = jnp.where(x < 0.25, x * series, 1.0 - jnp.exp(-x))
    return residue * jnp.sqrt(one_minus)


def block_kernel(
    nctx,
    ngrp,
    doc_hbm,
    q_hbm,
    k_hbm,
    v_hbm,
    taps_hbm,
    rate_hbm,
    res_hbm,
    resid_hbm,
    gain_hbm,
    hid_hbm,
    norm_hbm,
    doc_ref,
    q_ref,
    k_ref,
    v_ref,
    taps_ref,
    rate_ref,
    res_ref,
    resid_ref,
    gain_ref,
    hid_ref,
    norm_ref,
    tail_ref,
    halo_ref,
    qs_ref,
    g_ref,
    y_ref,
    keep_ref,
    pre_ref,
    late_ref,
    carry_ref,
    nat_ref,
    a_ref,
    w_ref,
    rate3_ref,
    e_ref,
    r1_ref,
    t_ref,
    r2_ref,
    i_ref,
    r3_ref,
    ss_ref,
    rs_ref,
    load_sem,
    store_sem,
    halo_send,
    halo_recv,
    s1,
    v1,
    s2,
    v2,
    s3,
    v3,
    s4,
    v4,
    ready,
):
    tok, chans = q_ref.shape
    lanes = 128
    sub = 8
    chunks = tok // sub
    tiles = chans // lanes
    modes = rate_ref.shape[0]
    ndoc = doc_ref.shape[0]
    quarter = modes // YN
    zn = nctx // YN
    me = lax.axis_index("ctx")
    gi = lax.axis_index("grp")
    z = me // YN
    yy = lax.rem(me, YN)

    def in_plane(k):
        return z * YN + lax.rem(yy + k, YN)

    def plane(k):
        return (z + k) * YN + yy

    barrier = pltpu.get_barrier_semaphore()
    @pl.when(me > 0)
    def _():
        pl.semaphore_signal(barrier, inc=1, device_id={"ctx": me - 1}, device_id_type=MESH)

    for k in range(1, YN):
        pl.semaphore_signal(
            barrier, inc=1, device_id={"ctx": in_plane(YN - k)}, device_id_type=MESH
        )
    for k in range(1, BACK + 1):

        @pl.when(z + k < zn)
        def _(k=k):
            pl.semaphore_signal(barrier, inc=1, device_id={"ctx": plane(k)}, device_id_type=MESH)

    for k in range(1, ngrp):
        pl.semaphore_signal(
            barrier, inc=1, device_id={"grp": lax.rem(gi + ngrp - k, ngrp)}, device_id_type=MESH
        )

    pairs = (
        (doc_hbm, doc_ref),
        (k_hbm, k_ref),
        (v_hbm, v_ref),
        (q_hbm, q_ref),
        (rate_hbm, rate_ref),
        (taps_hbm, taps_ref),
        (res_hbm, res_ref),
        (resid_hbm, resid_ref),
        (gain_hbm, gain_ref),
    )
    loads = [
        pltpu.make_async_copy(src, dst, load_sem.at[i]) for i, (src, dst) in enumerate(pairs)
    ]
    for copy in loads:
        copy.start()

    loads[0].wait()
    row = lax.broadcasted_iota(jnp.int32, (tok, lanes), 0)
    p0 = me * tok
    start = jnp.int32(0)
    first = jnp.int32(tok)
    last = jnp.int32(-1)
    before = jnp.int32(0)
    fresh = jnp.zeros((tok, lanes), F32)
    for d in range(ndoc):
        rel = start - p0
        fresh = jnp.where(row == rel, 1.0, fresh)
        before = jnp.where(rel == -1, 1, before)
        first = jnp.where(rel >= 0, jnp.minimum(first, rel), first)
        last = jnp.where((rel >= 0) & (rel < tok), rel, last)
        start = start + doc_ref[d]
    keep_one = 1.0 - fresh
    keep_ref[...] = keep_one
    keep_prev = jnp.where(row == 0, (1 - before).astype(F32), pltpu.roll(keep_one, 1, 0))
    keep_two = keep_one * keep_prev
    pre_ref[...] = jnp.where(row < first, 1.0, 0.0)
    late_ref[...] = jnp.where(row >= last, 1.0, 0.0)

    for copy in loads[1:4]:
        copy.wait()
    for i, ref in enumerate((q_ref, k_ref, v_ref)):
        tail_ref[2 * i : 2 * i + 2, :] = ref[tok - 16 :, :].astype(F32)[14:16]
    tail_ref[6:8, :] = jnp.zeros((2, chans), F32)
    for copy in loads[4:]:
        copy.wait()

    def by_mode(slot, value, dest):
        for j in range(tiles):
            nat_ref[slot, j * modes : (j + 1) * modes, :] = value[:, j * lanes : (j + 1) * lanes]
        for n in range(modes):
            dest[n] = nat_ref[slot, pl.ds(n, tiles, stride=modes), :]

    rate = rate_ref[...]
    by_mode(0, jnp.exp(-rate), a_ref)
    by_mode(2, rate, rate3_ref)

    def short(ref, i, j, rows, rim):
        cols = slice(j * lanes, (j + 1) * lanes)
        x = (ref[:, cols] if rows == tok else ref[0:16, cols]).astype(F32)[0:rows]
        one = pltpu.roll(x, 1, 0)
        two = pltpu.roll(x, 2, 0)
        if rim:
            at = row[0:rows]
            h0 = halo_ref[2 * i : 2 * i + 1, cols]
            h1 = halo_ref[2 * i + 1 : 2 * i + 2, cols]
            one = jnp.where(at == 0, h1, one)
            two = jnp.where(at == 0, h0, jnp.where(at == 1, h1, two))
        return (
            taps_ref[i, 0:1, cols] * x
            + taps_ref[i, 1:2, cols] * (one * keep_one[0:rows])
            + taps_ref[i, 2:3, cols] * (two * keep_two[0:rows])
        )

    for j in range(tiles):
        gate = short(k_ref, 1, j, tok, False) * short(v_ref, 2, j, tok, False)
        gate = gate.astype(BF16).astype(F32).reshape(chunks, sub, lanes)
        g_ref[:, j * sub : (j + 1) * sub, :] = gate

    def gate_at(c, r):
        return g_ref[c, pl.ds(r, tiles, stride=sub), :]

    def late_gate(c, r):
        return gate_at(c, r) * late_ref[pl.ds(c * sub + r, 1), :]

    greeted = (YN - 1) + (ngrp - 1) + jnp.minimum(z, BACK) + jnp.minimum(nctx - 1 - me, 1)
    pl.semaphore_wait(barrier, greeted)
    halo = pltpu.make_async_remote_copy(
        src_ref=tail_ref,
        dst_ref=halo_ref,
        send_sem=halo_send,
        recv_sem=halo_recv,
        device_id={"ctx": me + 1},
        device_id_type=MESH,
    )

    @pl.when(me < nctx - 1)
    def _():
        halo.start()

    @pl.when(me == 0)
    def _():
        halo_ref[...] = jnp.zeros_like(halo_ref)

    for k in range(1, BACK + 1):

        @pl.when(z >= k)
        def _(k=k):
            pl.semaphore_signal(ready, inc=1, device_id={"ctx": plane(-k)}, device_id_type=MESH)

    def end_chunk(c, states, first_row=0):
        for r in range(first_row, sub):
            g = late_gate(c, r)
            states = tuple(a_ref[n] * states[n] + g for n in range(modes))
        return states

    zero = jnp.zeros((tiles, lanes), F32)
    states = end_chunk(0, (zero,) * modes, 2)
    states = lax.fori_loop(1, chunks, end_chunk, states)
    for n in range(modes):
        e_ref[n] = states[n]

    by_mode(1, decay_weight(rate, res_ref[...]), w_ref)
    brow = lax.broadcasted_iota(jnp.int32, (nctx, lanes), 0)
    opens = jnp.zeros((nctx, lanes), F32)
    start = jnp.int32(0)
    for d in range(ndoc):
        opens = jnp.where(brow == start // tok, 1.0, opens)
        start = start + doc_ref[d]
    carry_ref[...] = 1.0 - opens
    @pl.when(me > 0)
    def _():
        halo.wait_recv()

    for j in range(tiles):
        gate = short(k_ref, 1, j, sub, True) * short(v_ref, 2, j, sub, True)
        g_ref[0, j * sub : (j + 1) * sub, :] = gate.astype(BF16).astype(F32)
    g0 = late_gate(0, 0)
    g1 = late_gate(0, 1)
    for n in range(modes):
        e_ref[n] = e_ref[n] + jnp.exp(-float(tok - 2) * rate3_ref[n]) * (g1 + a_ref[n] * g0)

    sends = []
    for k in range(1, YN):
        to = lax.rem(yy + k, YN)
        sends.append(
            pltpu.make_async_remote_copy(
                src_ref=e_ref.at[pl.ds(to * quarter, quarter)],
                dst_ref=r1_ref.at[k],
                send_sem=s1.at[k],
                recv_sem=v1.at[k],
                device_id={"ctx": in_plane(k)},
                device_id_type=MESH,
            )
        )
    for copy in sends:
        copy.start()
    r1_ref[0] = e_ref[pl.ds(yy * quarter, quarter)]
    rate_q = rate3_ref[pl.ds(yy * quarter, quarter)]
    decay_blk = jnp.exp(-float(tok) * rate_q)
    decay_plane = jnp.exp(-float(tok * YN) * rate_q)

    def carry_of(block):
        return carry_ref[pl.ds(block, 1), :][None]

    def plane_carry(k):
        base = lax.rem(z - k + zn, zn) * YN
        value = carry_of(base)
        for j in range(1, YN):
            value = value * carry_of(base + j)
        return value

    def scan_chunk(c, states):
        for r in range(sub):
            g = gate_at(c, r)
            keep = keep_ref[pl.ds(c * sub + r, 1), :]
            new = []
            total = None
            for n in range(modes):
                s = a_ref[n] * (keep * states[n]) + g
                term = w_ref[n] * s
                total = term if total is None else total + term
                new.append(s)
            y_ref[c, pl.ds(r, tiles, stride=sub), :] = total
            states = tuple(new)
        return states

    states = lax.fori_loop(0, chunks // 4, scan_chunk, (zero,) * modes)

    for copy in sends:
        copy.wait()

    ends = [r1_ref[lax.rem(yy - j + YN, YN)] for j in range(YN)]
    total = ends[0]
    for j in range(1, YN):
        total = ends[j] + decay_blk * carry_of(z * YN + j) * total
    t_ref[...] = total

    sends = []
    for k in range(1, BACK + 1):
        sends.append(
            pltpu.make_async_remote_copy(
                src_ref=t_ref,
                dst_ref=r2_ref.at[k - 1],
                send_sem=s2.at[k - 1],
                recv_sem=v2.at[k - 1],
                device_id={"ctx": plane(k)},
                device_id_type=MESH,
            )
        )
    totals = sends
    @pl.when(z < zn - 1)
    def _():
        pl.semaphore_wait(ready, jnp.minimum(zn - 1 - z, BACK))

    for k in range(BACK, 0, -1):

        @pl.when(z + k < zn)
        def _(k=k):
            totals[k - 1].start()

        @pl.when(z < k)
        def _(k=k):
            r2_ref[k - 1] = jnp.zeros(t_ref.shape, F32)

    lax.fori_loop(chunks // 4, chunks, scan_chunk, states)
    for j in range(tiles):
        cols = slice(j * lanes, (j + 1) * lanes)
        qs_ref[:, cols] = short(q_ref, 0, j, tok, True)
    for k in range(1, BACK + 1):

        @pl.when(z >= k)
        def _(k=k):
            totals[k - 1].wait_recv()

    enter = r2_ref[BACK - 1]
    for k in range(BACK - 1, 0, -1):
        enter = r2_ref[k - 1] + decay_plane * plane_carry(k) * enter
    for j in range(YN):
        i_ref[j] = enter
        if j < YN - 1:
            enter = ends[j] + decay_blk * carry_of(z * YN + j) * enter

    sends = []
    for k in range(1, YN):
        to = lax.rem(yy + k, YN)
        sends.append(
            pltpu.make_async_remote_copy(
                src_ref=i_ref.at[to],
                dst_ref=r3_ref.at[k],
                send_sem=s3.at[k],
                recv_sem=v3.at[k],
                device_id={"ctx": in_plane(k)},
                device_id_type=MESH,
            )
        )
    for copy in sends:
        copy.start()
    r3_ref[0] = i_ref[yy]
    for copy in sends:
        copy.wait()

    entering = []
    for m in range(YN):
        part = r3_ref[lax.rem(yy - m + YN, YN)]
        for n in range(quarter):
            entering.append(w_ref[m * quarter + n] * part[n])

    def fix_chunk(c, states):
        for r in range(sub):
            states = tuple(a_ref[n] * states[n] for n in range(modes))
            total = states[0]
            for n in range(1, modes):
                total = total + states[n]
            at = pl.ds(r, tiles, stride=sub)
            y_ref[c, at, :] = y_ref[c, at, :] + pre_ref[pl.ds(c * sub + r, 1), :] * total
        return states

    lax.fori_loop(0, chunks, fix_chunk, tuple(entering))

    squares = jnp.zeros((tok, lanes), F32)
    for j in range(tiles):
        cols = slice(j * lanes, (j + 1) * lanes)
        conv = y_ref[:, j * sub : (j + 1) * sub, :].reshape(tok, lanes)
        conv = conv.astype(BF16).astype(F32)
        hidden = resid_ref[:, cols].astype(F32) + qs_ref[:, cols] * conv
        squares = squares + hidden * hidden
        qs_ref[:, cols] = hidden
    by_token = jnp.sum(squares.T, axis=0, keepdims=True)
    ss_ref[...] = jnp.broadcast_to(by_token, (8, lanes))
    sends = []
    for k in range(1, ngrp):
        sends.append(
            pltpu.make_async_remote_copy(
                src_ref=ss_ref,
                dst_ref=rs_ref.at[k],
                send_sem=s4.at[k],
                recv_sem=v4.at[k],
                device_id={"grp": lax.rem(gi + k, ngrp)},
                device_id_type=MESH,
            )
        )
    for copy in sends:
        copy.start()
    hid_ref[...] = qs_ref[...].astype(BF16)
    hid_out = pltpu.make_async_copy(hid_ref, hid_hbm, store_sem.at[0])
    hid_out.start()
    for copy in sends:
        copy.wait()
    total = ss_ref[...]
    for k in range(1, ngrp):
        total = total + rs_ref[k]
    inverse = lax.rsqrt(total * (1.0 / D) + 1e-06)
    inverse = jnp.broadcast_to(inverse[0:1, :], (lanes, tok)).T
    for j in range(tiles):
        cols = slice(j * lanes, (j + 1) * lanes)
        norm_ref[:, cols] = (qs_ref[:, cols] * inverse * gain_ref[:, cols]).astype(BF16)
    norm_out = pltpu.make_async_copy(norm_ref, norm_hbm, store_sem.at[1])
    norm_out.start()

    @pl.when(me < nctx - 1)
    def _():
        halo.wait_send()

    for k in range(1, BACK + 1):

        @pl.when(z + k < zn)
        def _(k=k):
            totals[k - 1].wait_send()

    hid_out.wait()
    norm_out.wait()


def shards(
    nctx,
    ngrp,
    query_in,
    key_in,
    value_in,
    short_taps,
    decay_rate,
    residues,
    doc_lengths,
    residual,
    norm_gain,
):
    tok, chans = query_in.shape
    modes = decay_rate.shape[0]
    tiles = chans // 128
    quarter = modes // YN
    anywhere = pl.BlockSpec(memory_space=pl.ANY)
    state = (modes, tiles, 128)
    part = (quarter, tiles, 128)
    chunked = (tok // 8, tiles * 8, 128)
    dma = pltpu.SemaphoreType.DMA
    return pl.pallas_call(
        functools.partial(block_kernel, nctx, ngrp),
        out_shape=(
            jax.ShapeDtypeStruct((tok, chans), BF16),
            jax.ShapeDtypeStruct((tok, chans), BF16),
        ),
        in_specs=[anywhere] * 9,
        out_specs=(anywhere, anywhere),
        scratch_shapes=[
            pltpu.SMEM(doc_lengths.shape, jnp.int32),
            pltpu.VMEM((tok, chans), BF16),
            pltpu.VMEM((tok, chans), BF16),
            pltpu.VMEM((tok, chans), BF16),
            pltpu.VMEM(short_taps.shape, F32),
            pltpu.VMEM(decay_rate.shape, F32),
            pltpu.VMEM(residues.shape, F32),
            pltpu.VMEM((tok, chans), BF16),
            pltpu.VMEM((1, chans), F32),
            pltpu.VMEM((tok, chans), BF16),
            pltpu.VMEM((tok, chans), BF16),
            pltpu.VMEM((8, chans), F32),
            pltpu.VMEM((8, chans), F32),
            pltpu.VMEM((tok, chans), F32),
            pltpu.VMEM(chunked, F32),
            pltpu.VMEM(chunked, F32),
            pltpu.VMEM((tok, 128), F32),
            pltpu.VMEM((tok, 128), F32),
            pltpu.VMEM((tok, 128), F32),
            pltpu.VMEM((nctx, 128), F32),
            pltpu.VMEM((3, tiles * modes, 128), F32),
            pltpu.VMEM(state, F32),
            pltpu.VMEM(state, F32),
            pltpu.VMEM(state, F32),
            pltpu.VMEM(state, F32),
            pltpu.VMEM((YN,) + part, F32),
            pltpu.VMEM(part, F32),
            pltpu.VMEM((BACK,) + part, F32),
            pltpu.VMEM((YN,) + part, F32),
            pltpu.VMEM((YN,) + part, F32),
            pltpu.VMEM((8, 128), F32),
            pltpu.VMEM((ngrp, 8, 128), F32),
            dma((9,)),
            dma((2,)),
            dma,
            dma,
            dma((YN,)),
            dma((YN,)),
            dma((BACK,)),
            dma((BACK,)),
            dma((YN,)),
            dma((YN,)),
            dma((ngrp,)),
            dma((ngrp,)),
            pltpu.SemaphoreType.REGULAR,
        ],
        compiler_params=pltpu.CompilerParams(collective_id=0, has_side_effects=True),
        name="hyena_block",
    )(
        doc_lengths,
        query_in,
        key_in,
        value_in,
        short_taps,
        decay_rate,
        residues,
        residual,
        norm_gain.reshape(1, chans),
    )


def solution(mesh):
    return jax.shard_map(
        functools.partial(shards, mesh.shape["ctx"], mesh.shape["grp"]),
        mesh=mesh,
        in_specs=(
            P("ctx", "grp"),
            P("ctx", "grp"),
            P("ctx", "grp"),
            P(None, None, "grp"),
            P(None, "grp"),
            P(None, "grp"),
            P(),
            P("ctx", "grp"),
            P("grp"),
        ),
        out_specs=(P("ctx", "grp"), P("ctx", "grp")),
        check_vma=False,
    )
```

```python
import functools

import jax
import jax.numpy as jnp
from jax import lax
from jax.experimental import pallas as pl
from jax.experimental.pallas import tpu as pltpu
from jax.sharding import PartitionSpec as P

D = 8192
MESH = pl.DeviceIdType.MESH
F32 = jnp.float32
BF16 = jnp.bfloat16
YN = 4
BACK = 4


def decay_weight(rate, residue):
    x = 2.0 * rate
    series = 1.0 - x / 8.0
    for k in (7.0, 6.0, 5.0, 4.0, 3.0, 2.0):
        series = 1.0 - (x / k) * series
    one_minus = jnp.where(x < 0.25, x * series, 1.0 - jnp.exp(-x))
    return residue * jnp.sqrt(one_minus)


def block_kernel(
    nctx,
    ngrp,
    doc_hbm,
    q_hbm,
    k_hbm,
    v_hbm,
    taps_hbm,
    rate_hbm,
    res_hbm,
    resid_hbm,
    hid_hbm,
    inv_hbm,
    doc_ref,
    q_ref,
    k_ref,
    v_ref,
    taps_ref,
    rate_ref,
    res_ref,
    resid_ref,
    inv_ref,
    tail_ref,
    halo_ref,
    qs_ref,
    g_ref,
    y_ref,
    keep_ref,
    pre_ref,
    late_ref,
    carry_ref,
    nat_ref,
    a_ref,
    w_ref,
    rate3_ref,
    e_ref,
    r1_ref,
    t_ref,
    r2_ref,
    i_ref,
    r3_ref,
    ss_ref,
    rs_ref,
    load_sem,
    store_sem,
    halo_send,
    halo_recv,
    s1,
    v1,
    s2,
    v2,
    s3,
    v3,
    s4,
    v4,
    ready,
):
    tok, chans = q_ref.shape
    lanes = 128
    sub = 8
    chunks = tok // sub
    tiles = chans // lanes
    modes = rate_ref.shape[0]
    ndoc = doc_ref.shape[0]
    quarter = modes // YN
    zn = nctx // YN
    me = lax.axis_index("ctx")
    gi = lax.axis_index("grp")
    z = me // YN
    yy = lax.rem(me, YN)

    def in_plane(k):
        return z * YN + lax.rem(yy + k, YN)

    def plane(k):
        return (z + k) * YN + yy

    barrier = pltpu.get_barrier_semaphore()
    @pl.when(me > 0)
    def _():
        pl.semaphore_signal(barrier, inc=1, device_id={"ctx": me - 1}, device_id_type=MESH)

    for k in range(1, YN):
        pl.semaphore_signal(
            barrier, inc=1, device_id={"ctx": in_plane(YN - k)}, device_id_type=MESH
        )
    for k in range(1, BACK + 1):

        @pl.when(z + k < zn)
        def _(k=k):
            pl.semaphore_signal(barrier, inc=1, device_id={"ctx": plane(k)}, device_id_type=MESH)

    for k in range(1, ngrp):
        pl.semaphore_signal(
            barrier, inc=1, device_id={"grp": lax.rem(gi + ngrp - k, ngrp)}, device_id_type=MESH
        )

    pairs = (
        (doc_hbm, doc_ref),
        (k_hbm, k_ref),
        (v_hbm, v_ref),
        (q_hbm, q_ref),
        (rate_hbm, rate_ref),
        (taps_hbm, taps_ref),
        (res_hbm, res_ref),
        (resid_hbm, resid_ref),
    )
    loads = [
        pltpu.make_async_copy(src, dst, load_sem.at[i]) for i, (src, dst) in enumerate(pairs)
    ]
    for copy in loads:
        copy.start()

    loads[0].wait()
    row = lax.broadcasted_iota(jnp.int32, (tok, lanes), 0)
    p0 = me * tok
    start = jnp.int32(0)
    first = jnp.int32(tok)
    last = jnp.int32(-1)
    before = jnp.int32(0)
    fresh = jnp.zeros((tok, lanes), F32)
    for d in range(ndoc):
        rel = start - p0
        fresh = jnp.where(row == rel, 1.0, fresh)
        before = jnp.where(rel == -1, 1, before)
        first = jnp.where(rel >= 0, jnp.minimum(first, rel), first)
        last = jnp.where((rel >= 0) & (rel < tok), rel, last)
        start = start + doc_ref[d]
    keep_one = 1.0 - fresh
    keep_ref[...] = keep_one
    keep_prev = jnp.where(row == 0, (1 - before).astype(F32), pltpu.roll(keep_one, 1, 0))
    keep_two = keep_one * keep_prev
    pre_ref[...] = jnp.where(row < first, 1.0, 0.0)
    late_ref[...] = jnp.where(row >= last, 1.0, 0.0)

    for copy in loads[1:4]:
        copy.wait()
    for i, ref in enumerate((q_ref, k_ref, v_ref)):
        tail_ref[2 * i : 2 * i + 2, :] = ref[tok - 16 :, :].astype(F32)[14:16]
    tail_ref[6:8, :] = jnp.zeros((2, chans), F32)
    for copy in loads[4:]:
        copy.wait()

    def by_mode(slot, value, dest):
        for j in range(tiles):
            nat_ref[slot, j * modes : (j + 1) * modes, :] = value[:, j * lanes : (j + 1) * lanes]
        for n in range(modes):
            dest[n] = nat_ref[slot, pl.ds(n, tiles, stride=modes), :]

    rate = rate_ref[...]
    by_mode(0, jnp.exp(-rate), a_ref)
    by_mode(2, rate, rate3_ref)

    def short(ref, i, j, rows, rim):
        cols = slice(j * lanes, (j + 1) * lanes)
        x = (ref[:, cols] if rows == tok else ref[0:16, cols]).astype(F32)[0:rows]
        one = pltpu.roll(x, 1, 0)
        two = pltpu.roll(x, 2, 0)
        if rim:
            at = row[0:rows]
            h0 = halo_ref[2 * i : 2 * i + 1, cols]
            h1 = halo_ref[2 * i + 1 : 2 * i + 2, cols]
            one = jnp.where(at == 0, h1, one)
            two = jnp.where(at == 0, h0, jnp.where(at == 1, h1, two))
        return (
            taps_ref[i, 0:1, cols] * x
            + taps_ref[i, 1:2, cols] * (one * keep_one[0:rows])
            + taps_ref[i, 2:3, cols] * (two * keep_two[0:rows])
        )

    for j in range(tiles):
        gate = short(k_ref, 1, j, tok, False) * short(v_ref, 2, j, tok, False)
        gate = gate.astype(BF16).astype(F32).reshape(chunks, sub, lanes)
        g_ref[:, j * sub : (j + 1) * sub, :] = gate

    def gate_at(c, r):
        return g_ref[c, pl.ds(r, tiles, stride=sub), :]

    def late_gate(c, r):
        return gate_at(c, r) * late_ref[pl.ds(c * sub + r, 1), :]

    greeted = (YN - 1) + (ngrp - 1) + jnp.minimum(z, BACK) + jnp.minimum(nctx - 1 - me, 1)
    pl.semaphore_wait(barrier, greeted)
    halo = pltpu.make_async_remote_copy(
        src_ref=tail_ref,
        dst_ref=halo_ref,
        send_sem=halo_send,
        recv_sem=halo_recv,
        device_id={"ctx": me + 1},
        device_id_type=MESH,
    )

    @pl.when(me < nctx - 1)
    def _():
        halo.start()

    @pl.when(me == 0)
    def _():
        halo_ref[...] = jnp.zeros_like(halo_ref)

    for k in range(1, BACK + 1):

        @pl.when(z >= k)
        def _(k=k):
            pl.semaphore_signal(ready, inc=1, device_id={"ctx": plane(-k)}, device_id_type=MESH)

    def end_chunk(c, states, first_row=0):
        for r in range(first_row, sub):
            g = late_gate(c, r)
            states = tuple(a_ref[n] * states[n] + g for n in range(modes))
        return states

    zero = jnp.zeros((tiles, lanes), F32)
    states = end_chunk(0, (zero,) * modes, 2)
    states = lax.fori_loop(1, chunks, end_chunk, states)
    for n in range(modes):
        e_ref[n] = states[n]

    by_mode(1, decay_weight(rate, res_ref[...]), w_ref)
    brow = lax.broadcasted_iota(jnp.int32, (nctx, lanes), 0)
    opens = jnp.zeros((nctx, lanes), F32)
    start = jnp.int32(0)
    for d in range(ndoc):
        opens = jnp.where(brow == start // tok, 1.0, opens)
        start = start + doc_ref[d]
    carry_ref[...] = 1.0 - opens
    @pl.when(me > 0)
    def _():
        halo.wait_recv()

    for j in range(tiles):
        gate = short(k_ref, 1, j, sub, True) * short(v_ref, 2, j, sub, True)
        g_ref[0, j * sub : (j + 1) * sub, :] = gate.astype(BF16).astype(F32)
    g0 = late_gate(0, 0)
    g1 = late_gate(0, 1)
    for n in range(modes):
        e_ref[n] = e_ref[n] + jnp.exp(-float(tok - 2) * rate3_ref[n]) * (g1 + a_ref[n] * g0)

    sends = []
    for k in range(1, YN):
        to = lax.rem(yy + k, YN)
        sends.append(
            pltpu.make_async_remote_copy(
                src_ref=e_ref.at[pl.ds(to * quarter, quarter)],
                dst_ref=r1_ref.at[k],
                send_sem=s1.at[k],
                recv_sem=v1.at[k],
                device_id={"ctx": in_plane(k)},
                device_id_type=MESH,
            )
        )
    for copy in sends:
        copy.start()
    r1_ref[0] = e_ref[pl.ds(yy * quarter, quarter)]
    rate_q = rate3_ref[pl.ds(yy * quarter, quarter)]
    decay_blk = jnp.exp(-float(tok) * rate_q)
    decay_plane = jnp.exp(-float(tok * YN) * rate_q)

    def carry_of(block):
        return carry_ref[pl.ds(block, 1), :][None]

    def plane_carry(k):
        base = lax.rem(z - k + zn, zn) * YN
        value = carry_of(base)
        for j in range(1, YN):
            value = value * carry_of(base + j)
        return value

    def scan_chunk(c, states):
        for r in range(sub):
            g = gate_at(c, r)
            keep = keep_ref[pl.ds(c * sub + r, 1), :]
            new = []
            total = None
            for n in range(modes):
                s = a_ref[n] * (keep * states[n]) + g
                term = w_ref[n] * s
                total = term if total is None else total + term
                new.append(s)
            y_ref[c, pl.ds(r, tiles, stride=sub), :] = total
            states = tuple(new)
        return states

    states = lax.fori_loop(0, chunks // 2, scan_chunk, (zero,) * modes)

    for copy in sends:
        copy.wait()

    ends = [r1_ref[lax.rem(yy - j + YN, YN)] for j in range(YN)]
    total = ends[0]
    for j in range(1, YN):
        total = ends[j] + decay_blk * carry_of(z * YN + j) * total
    t_ref[...] = total

    sends = []
    for k in range(1, BACK + 1):
        sends.append(
            pltpu.make_async_remote_copy(
                src_ref=t_ref,
                dst_ref=r2_ref.at[k - 1],
                send_sem=s2.at[k - 1],
                recv_sem=v2.at[k - 1],
                device_id={"ctx": plane(k)},
                device_id_type=MESH,
            )
        )
    totals = sends
    @pl.when(z < zn - 1)
    def _():
        pl.semaphore_wait(ready, jnp.minimum(zn - 1 - z, BACK))

    for k in range(BACK, 0, -1):

        @pl.when(z + k < zn)
        def _(k=k):
            totals[k - 1].start()

        @pl.when(z < k)
        def _(k=k):
            r2_ref[k - 1] = jnp.zeros(t_ref.shape, F32)

    for j in range(tiles):
        cols = slice(j * lanes, (j + 1) * lanes)
        qs_ref[:, cols] = short(q_ref, 0, j, tok, True)
    for k in range(1, BACK + 1):

        @pl.when(z >= k)
        def _(k=k):
            totals[k - 1].wait_recv()

    enter = r2_ref[BACK - 1]
    for k in range(BACK - 1, 0, -1):
        enter = r2_ref[k - 1] + decay_plane * plane_carry(k) * enter
    for j in range(YN):
        i_ref[j] = enter
        if j < YN - 1:
            enter = ends[j] + decay_blk * carry_of(z * YN + j) * enter

    sends = []
    for k in range(1, YN):
        to = lax.rem(yy + k, YN)
        sends.append(
            pltpu.make_async_remote_copy(
                src_ref=i_ref.at[to],
                dst_ref=r3_ref.at[k],
                send_sem=s3.at[k],
                recv_sem=v3.at[k],
                device_id={"ctx": in_plane(k)},
                device_id_type=MESH,
            )
        )
    for copy in sends:
        copy.start()
    r3_ref[0] = i_ref[yy]
    lax.fori_loop(chunks // 2, chunks, scan_chunk, states)
    for copy in sends:
        copy.wait()

    entering = []
    for m in range(YN):
        part = r3_ref[lax.rem(yy - m + YN, YN)]
        for n in range(quarter):
            entering.append(w_ref[m * quarter + n] * part[n])

    def fix_chunk(c, states):
        for r in range(sub):
            states = tuple(a_ref[n] * states[n] for n in range(modes))
            total = states[0]
            for n in range(1, modes):
                total = total + states[n]
            at = pl.ds(r, tiles, stride=sub)
            y_ref[c, at, :] = y_ref[c, at, :] + pre_ref[pl.ds(c * sub + r, 1), :] * total
        return states

    lax.fori_loop(0, chunks, fix_chunk, tuple(entering))

    squares = jnp.zeros((tok, lanes), F32)
    for j in range(tiles):
        cols = slice(j * lanes, (j + 1) * lanes)
        conv = y_ref[:, j * sub : (j + 1) * sub, :].reshape(tok, lanes)
        conv = conv.astype(BF16).astype(F32)
        hidden = resid_ref[:, cols].astype(F32) + qs_ref[:, cols] * conv
        squares = squares + hidden * hidden
        qs_ref[:, cols] = hidden
    by_token = jnp.sum(squares.T, axis=0, keepdims=True)
    ss_ref[...] = jnp.broadcast_to(by_token, (8, lanes))
    sends = []
    for k in range(1, ngrp):
        sends.append(
            pltpu.make_async_remote_copy(
                src_ref=ss_ref,
                dst_ref=rs_ref.at[k],
                send_sem=s4.at[k],
                recv_sem=v4.at[k],
                device_id={"grp": lax.rem(gi + k, ngrp)},
                device_id_type=MESH,
            )
        )
    for copy in sends:
        copy.start()
    hid_out = pltpu.make_async_copy(qs_ref, hid_hbm, store_sem.at[0])
    hid_out.start()
    for copy in sends:
        copy.wait()
    total = ss_ref[...]
    for k in range(1, ngrp):
        total = total + rs_ref[k]
    inverse = lax.rsqrt(total * (1.0 / D) + 1e-06)
    inv_ref[...] = inverse[0:1, :]
    inv_out = pltpu.make_async_copy(inv_ref, inv_hbm, store_sem.at[1])
    inv_out.start()

    @pl.when(me < nctx - 1)
    def _():
        halo.wait_send()

    for k in range(1, BACK + 1):

        @pl.when(z + k < zn)
        def _(k=k):
            totals[k - 1].wait_send()

    hid_out.wait()
    inv_out.wait()


def shards(
    nctx,
    ngrp,
    query_in,
    key_in,
    value_in,
    short_taps,
    decay_rate,
    residues,
    doc_lengths,
    residual,
    norm_gain,
):
    tok, chans = query_in.shape
    modes = decay_rate.shape[0]
    tiles = chans // 128
    quarter = modes // YN
    anywhere = pl.BlockSpec(memory_space=pl.ANY)
    state = (modes, tiles, 128)
    part = (quarter, tiles, 128)
    chunked = (tok // 8, tiles * 8, 128)
    dma = pltpu.SemaphoreType.DMA
    hidden, inverse = pl.pallas_call(
        functools.partial(block_kernel, nctx, ngrp),
        out_shape=(
            jax.ShapeDtypeStruct((tok, chans), F32),
            jax.ShapeDtypeStruct((1, tok), F32),
        ),
        in_specs=[anywhere] * 8,
        out_specs=(anywhere, anywhere),
        scratch_shapes=[
            pltpu.SMEM(doc_lengths.shape, jnp.int32),
            pltpu.VMEM((tok, chans), BF16),
            pltpu.VMEM((tok, chans), BF16),
            pltpu.VMEM((tok, chans), BF16),
            pltpu.VMEM(short_taps.shape, F32),
            pltpu.VMEM(decay_rate.shape, F32),
            pltpu.VMEM(residues.shape, F32),
            pltpu.VMEM((tok, chans), BF16),
            pltpu.VMEM((1, tok), F32),
            pltpu.VMEM((8, chans), F32),
            pltpu.VMEM((8, chans), F32),
            pltpu.VMEM((tok, chans), F32),
            pltpu.VMEM(chunked, F32),
            pltpu.VMEM(chunked, F32),
            pltpu.VMEM((tok, 128), F32),
            pltpu.VMEM((tok, 128), F32),
            pltpu.VMEM((tok, 128), F32),
            pltpu.VMEM((nctx, 128), F32),
            pltpu.VMEM((3, tiles * modes, 128), F32),
            pltpu.VMEM(state, F32),
            pltpu.VMEM(state, F32),
            pltpu.VMEM(state, F32),
            pltpu.VMEM(state, F32),
            pltpu.VMEM((YN,) + part, F32),
            pltpu.VMEM(part, F32),
            pltpu.VMEM((BACK,) + part, F32),
            pltpu.VMEM((YN,) + part, F32),
            pltpu.VMEM((YN,) + part, F32),
            pltpu.VMEM((8, 128), F32),
            pltpu.VMEM((ngrp, 8, 128), F32),
            dma((8,)),
            dma((2,)),
            dma,
            dma,
            dma((YN,)),
            dma((YN,)),
            dma((BACK,)),
            dma((BACK,)),
            dma((YN,)),
            dma((YN,)),
            dma((ngrp,)),
            dma((ngrp,)),
            pltpu.SemaphoreType.REGULAR,
        ],
        compiler_params=pltpu.CompilerParams(collective_id=0, has_side_effects=True),
        name="hyena_block",
    )(
        doc_lengths,
        query_in,
        key_in,
        value_in,
        short_taps,
        decay_rate,
        residues,
        residual,
    )
    normed = (hidden * inverse.reshape(tok)[:, None] * norm_gain[None, :]).astype(BF16)
    return (hidden.astype(BF16), normed)


def solution(mesh):
    return jax.shard_map(
        functools.partial(shards, mesh.shape["ctx"], mesh.shape["grp"]),
        mesh=mesh,
        in_specs=(
            P("ctx", "grp"),
            P("ctx", "grp"),
            P("ctx", "grp"),
            P(None, None, "grp"),
            P(None, "grp"),
            P(None, "grp"),
            P(),
            P("ctx", "grp"),
            P("grp"),
        ),
        out_specs=(P("ctx", "grp"), P("ctx", "grp")),
        check_vma=False,
    )
```

```python
import functools

import jax
import jax.numpy as jnp
from jax import lax
from jax.experimental import pallas as pl
from jax.experimental.pallas import tpu as pltpu
from jax.sharding import PartitionSpec as P

D = 8192
MESH = pl.DeviceIdType.MESH
F32 = jnp.float32
BF16 = jnp.bfloat16
YN = 4
BACK = 4


def decay_weight(rate, residue):
    x = 2.0 * rate
    series = 1.0 - x / 8.0
    for k in (7.0, 6.0, 5.0, 4.0, 3.0, 2.0):
        series = 1.0 - (x / k) * series
    one_minus = jnp.where(x < 0.25, x * series, 1.0 - jnp.exp(-x))
    return residue * jnp.sqrt(one_minus)


def block_kernel(
    nctx,
    ngrp,
    doc_hbm,
    q_hbm,
    k_hbm,
    v_hbm,
    taps_hbm,
    rate_hbm,
    res_hbm,
    resid_hbm,
    hid_hbm,
    inv_hbm,
    doc_ref,
    q_ref,
    k_ref,
    v_ref,
    taps_ref,
    rate_ref,
    res_ref,
    resid_ref,
    inv_ref,
    tail_ref,
    halo_ref,
    tail16_ref,
    halo16_ref,
    qs_ref,
    g_ref,
    y_ref,
    keep_ref,
    pre_ref,
    late_ref,
    carry_ref,
    nat_ref,
    a_ref,
    w_ref,
    rate3_ref,
    e_ref,
    r1_ref,
    t_ref,
    t16_ref,
    r2_ref,
    r216_ref,
    i_ref,
    r3_ref,
    ss_ref,
    rs_ref,
    load_sem,
    store_sem,
    halo_send,
    halo_recv,
    s1,
    v1,
    s2,
    v2,
    s3,
    v3,
    s4,
    v4,
    ready,
):
    tok, chans = q_ref.shape
    lanes = 128
    sub = 8
    chunks = tok // sub
    tiles = chans // lanes
    modes = rate_ref.shape[0]
    ndoc = doc_ref.shape[0]
    quarter = modes // YN
    zn = nctx // YN
    me = lax.axis_index("ctx")
    gi = lax.axis_index("grp")
    z = me // YN
    yy = lax.rem(me, YN)

    def in_plane(k):
        return z * YN + lax.rem(yy + k, YN)

    def plane(k):
        return (z + k) * YN + yy

    barrier = pltpu.get_barrier_semaphore()
    @pl.when(me > 0)
    def _():
        pl.semaphore_signal(barrier, inc=1, device_id={"ctx": me - 1}, device_id_type=MESH)

    for k in range(1, YN):
        pl.semaphore_signal(
            barrier, inc=1, device_id={"ctx": in_plane(YN - k)}, device_id_type=MESH
        )
    for k in range(1, BACK + 1):

        @pl.when(z + k < zn)
        def _(k=k):
            pl.semaphore_signal(barrier, inc=1, device_id={"ctx": plane(k)}, device_id_type=MESH)

    for k in range(1, ngrp):
        pl.semaphore_signal(
            barrier, inc=1, device_id={"grp": lax.rem(gi + ngrp - k, ngrp)}, device_id_type=MESH
        )

    pairs = (
        (doc_hbm, doc_ref),
        (k_hbm, k_ref),
        (v_hbm, v_ref),
        (q_hbm, q_ref),
        (rate_hbm, rate_ref),
        (taps_hbm, taps_ref),
        (res_hbm, res_ref),
        (resid_hbm, resid_ref),
    )
    loads = [
        pltpu.make_async_copy(src, dst, load_sem.at[i]) for i, (src, dst) in enumerate(pairs)
    ]
    for copy in loads:
        copy.start()

    loads[0].wait()
    row = lax.broadcasted_iota(jnp.int32, (tok, lanes), 0)
    p0 = me * tok
    start = jnp.int32(0)
    first = jnp.int32(tok)
    last = jnp.int32(-1)
    before = jnp.int32(0)
    fresh = jnp.zeros((tok, lanes), F32)
    for d in range(ndoc):
        rel = start - p0
        fresh = jnp.where(row == rel, 1.0, fresh)
        before = jnp.where(rel == -1, 1, before)
        first = jnp.where(rel >= 0, jnp.minimum(first, rel), first)
        last = jnp.where((rel >= 0) & (rel < tok), rel, last)
        start = start + doc_ref[d]
    keep_one = 1.0 - fresh
    keep_ref[...] = keep_one
    keep_prev = jnp.where(row == 0, (1 - before).astype(F32), pltpu.roll(keep_one, 1, 0))
    keep_two = keep_one * keep_prev
    pre_ref[...] = jnp.where(row < first, 1.0, 0.0)
    late_ref[...] = jnp.where(row >= last, 1.0, 0.0)

    for copy in loads[1:4]:
        copy.wait()
    for i, ref in enumerate((q_ref, k_ref, v_ref)):
        tail_ref[2 * i : 2 * i + 2, :] = ref[tok - 16 :, :].astype(F32)[14:16]
    tail_ref[6:8, :] = jnp.zeros((2, chans), F32)
    tail16_ref[...] = tail_ref[...].astype(BF16)
    for copy in loads[4:]:
        copy.wait()

    def by_mode(slot, value, dest):
        for j in range(tiles):
            nat_ref[slot, j * modes : (j + 1) * modes, :] = value[:, j * lanes : (j + 1) * lanes]
        for n in range(modes):
            dest[n] = nat_ref[slot, pl.ds(n, tiles, stride=modes), :]

    rate = rate_ref[...]
    by_mode(0, jnp.exp(-rate), a_ref)
    by_mode(2, rate, rate3_ref)

    def short(ref, i, j, rows, rim):
        cols = slice(j * lanes, (j + 1) * lanes)
        x = (ref[:, cols] if rows == tok else ref[0:16, cols]).astype(F32)[0:rows]
        one = pltpu.roll(x, 1, 0)
        two = pltpu.roll(x, 2, 0)
        if rim:
            at = row[0:rows]
            h0 = halo_ref[2 * i : 2 * i + 1, cols]
            h1 = halo_ref[2 * i + 1 : 2 * i + 2, cols]
            one = jnp.where(at == 0, h1, one)
            two = jnp.where(at == 0, h0, jnp.where(at == 1, h1, two))
        return (
            taps_ref[i, 0:1, cols] * x
            + taps_ref[i, 1:2, cols] * (one * keep_one[0:rows])
            + taps_ref[i, 2:3, cols] * (two * keep_two[0:rows])
        )

    for j in range(tiles):
        gate = short(k_ref, 1, j, tok, False) * short(v_ref, 2, j, tok, False)
        gate = gate.astype(BF16).astype(F32).reshape(chunks, sub, lanes)
        g_ref[:, j * sub : (j + 1) * sub, :] = gate

    def gate_at(c, r):
        return g_ref[c, pl.ds(r, tiles, stride=sub), :]

    def late_gate(c, r):
        return gate_at(c, r) * late_ref[pl.ds(c * sub + r, 1), :]

    greeted = (YN - 1) + (ngrp - 1) + jnp.minimum(z, BACK) + jnp.minimum(nctx - 1 - me, 1)
    pl.semaphore_wait(barrier, greeted)
    halo = pltpu.make_async_remote_copy(
        src_ref=tail16_ref,
        dst_ref=halo16_ref,
        send_sem=halo_send,
        recv_sem=halo_recv,
        device_id={"ctx": me + 1},
        device_id_type=MESH,
    )

    @pl.when(me < nctx - 1)
    def _():
        halo.start()

    @pl.when(me == 0)
    def _():
        halo16_ref[...] = jnp.zeros(halo16_ref.shape, BF16)

    for k in range(1, BACK + 1):

        @pl.when(z >= k)
        def _(k=k):
            pl.semaphore_signal(ready, inc=1, device_id={"ctx": plane(-k)}, device_id_type=MESH)

    def end_chunk(c, states, first_row=0):
        for r in range(first_row, sub):
            g = late_gate(c, r)
            states = tuple(a_ref[n] * states[n] + g for n in range(modes))
        return states

    zero = jnp.zeros((tiles, lanes), F32)
    states = end_chunk(0, (zero,) * modes, 2)
    states = lax.fori_loop(1, chunks, end_chunk, states)
    for n in range(modes):
        e_ref[n] = states[n]

    by_mode(1, decay_weight(rate, res_ref[...]), w_ref)
    brow = lax.broadcasted_iota(jnp.int32, (nctx, lanes), 0)
    opens = jnp.zeros((nctx, lanes), F32)
    start = jnp.int32(0)
    for d in range(ndoc):
        opens = jnp.where(brow == start // tok, 1.0, opens)
        start = start + doc_ref[d]
    carry_ref[...] = 1.0 - opens
    @pl.when(me > 0)
    def _():
        halo.wait_recv()

    halo_ref[...] = halo16_ref[...].astype(F32)
    for j in range(tiles):
        gate = short(k_ref, 1, j, sub, True) * short(v_ref, 2, j, sub, True)
        g_ref[0, j * sub : (j + 1) * sub, :] = gate.astype(BF16).astype(F32)
    g0 = late_gate(0, 0)
    g1 = late_gate(0, 1)
    for n in range(modes):
        e_ref[n] = e_ref[n] + jnp.exp(-float(tok - 2) * rate3_ref[n]) * (g1 + a_ref[n] * g0)

    sends = []
    for k in range(1, YN):
        to = lax.rem(yy + k, YN)
        sends.append(
            pltpu.make_async_remote_copy(
                src_ref=e_ref.at[pl.ds(to * quarter, quarter)],
                dst_ref=r1_ref.at[k],
                send_sem=s1.at[k],
                recv_sem=v1.at[k],
                device_id={"ctx": in_plane(k)},
                device_id_type=MESH,
            )
        )
    for copy in sends:
        copy.start()
    r1_ref[0] = e_ref[pl.ds(yy * quarter, quarter)]
    rate_q = rate3_ref[pl.ds(yy * quarter, quarter)]
    decay_blk = jnp.exp(-float(tok) * rate_q)
    decay_plane = jnp.exp(-float(tok * YN) * rate_q)

    def carry_of(block):
        return carry_ref[pl.ds(block, 1), :][None]

    def plane_carry(k):
        base = lax.rem(z - k + zn, zn) * YN
        value = carry_of(base)
        for j in range(1, YN):
            value = value * carry_of(base + j)
        return value

    def scan_chunk(c, states):
        for r in range(sub):
            g = gate_at(c, r)
            keep = keep_ref[pl.ds(c * sub + r, 1), :]
            new = []
            total = None
            for n in range(modes):
                s = a_ref[n] * (keep * states[n]) + g
                term = w_ref[n] * s
                total = term if total is None else total + term
                new.append(s)
            y_ref[c, pl.ds(r, tiles, stride=sub), :] = total
            states = tuple(new)
        return states

    states = lax.fori_loop(0, chunks // 2, scan_chunk, (zero,) * modes)

    for copy in sends:
        copy.wait()

    ends = [r1_ref[lax.rem(yy - j + YN, YN)] for j in range(YN)]
    total = ends[0]
    for j in range(1, YN):
        total = ends[j] + decay_blk * carry_of(z * YN + j) * total
    t_ref[...] = total
    t16_ref[...] = total.astype(BF16)

    sends = []
    for k in range(1, BACK + 1):
        sends.append(
            pltpu.make_async_remote_copy(
                src_ref=t_ref if k == 1 else t16_ref,
                dst_ref=r2_ref if k == 1 else r216_ref.at[k - 2],
                send_sem=s2.at[k - 1],
                recv_sem=v2.at[k - 1],
                device_id={"ctx": plane(k)},
                device_id_type=MESH,
            )
        )
    totals = sends
    @pl.when(z < zn - 1)
    def _():
        pl.semaphore_wait(ready, jnp.minimum(zn - 1 - z, BACK))

    for k in range(BACK, 0, -1):

        @pl.when(z + k < zn)
        def _(k=k):
            totals[k - 1].start()

        @pl.when(z < k)
        def _(k=k):
            if k == 1:
                r2_ref[...] = jnp.zeros(t_ref.shape, F32)
            else:
                r216_ref[k - 2] = jnp.zeros(t_ref.shape, BF16)

    states = lax.fori_loop(chunks // 2, 3 * chunks // 4, scan_chunk, states)
    for j in range(tiles):
        cols = slice(j * lanes, (j + 1) * lanes)
        qs_ref[:, cols] = short(q_ref, 0, j, tok, True)
    for k in range(1, BACK + 1):

        @pl.when(z >= k)
        def _(k=k):
            totals[k - 1].wait_recv()

    enter = r216_ref[BACK - 2].astype(F32)
    for k in range(BACK - 1, 0, -1):
        mine = r2_ref[...] if k == 1 else r216_ref[k - 2].astype(F32)
        enter = mine + decay_plane * plane_carry(k) * enter
    for j in range(YN):
        i_ref[j] = enter
        if j < YN - 1:
            enter = ends[j] + decay_blk * carry_of(z * YN + j) * enter

    sends = []
    for k in range(1, YN):
        to = lax.rem(yy + k, YN)
        sends.append(
            pltpu.make_async_remote_copy(
                src_ref=i_ref.at[to],
                dst_ref=r3_ref.at[k],
                send_sem=s3.at[k],
                recv_sem=v3.at[k],
                device_id={"ctx": in_plane(k)},
                device_id_type=MESH,
            )
        )
    for copy in sends:
        copy.start()
    r3_ref[0] = i_ref[yy]
    lax.fori_loop(3 * chunks // 4, chunks, scan_chunk, states)
    for copy in sends:
        copy.wait()

    entering = []
    for m in range(YN):
        part = r3_ref[lax.rem(yy - m + YN, YN)]
        for n in range(quarter):
            entering.append(w_ref[m * quarter + n] * part[n])

    def fix_chunk(c, states):
        for r in range(sub):
            states = tuple(a_ref[n] * states[n] for n in range(modes))
            total = states[0]
            for n in range(1, modes):
                total = total + states[n]
            at = pl.ds(r, tiles, stride=sub)
            y_ref[c, at, :] = y_ref[c, at, :] + pre_ref[pl.ds(c * sub + r, 1), :] * total
        return states

    lax.fori_loop(0, chunks, fix_chunk, tuple(entering))

    squares = jnp.zeros((tok, lanes), F32)
    for j in range(tiles):
        cols = slice(j * lanes, (j + 1) * lanes)
        conv = y_ref[:, j * sub : (j + 1) * sub, :].reshape(tok, lanes)
        conv = conv.astype(BF16).astype(F32)
        hidden = resid_ref[:, cols].astype(F32) + qs_ref[:, cols] * conv
        squares = squares + hidden * hidden
        qs_ref[:, cols] = hidden
    by_token = jnp.sum(squares.T, axis=0, keepdims=True)
    ss_ref[...] = jnp.broadcast_to(by_token, (8, lanes))
    sends = []
    for k in range(1, ngrp):
        sends.append(
            pltpu.make_async_remote_copy(
                src_ref=ss_ref,
                dst_ref=rs_ref.at[k],
                send_sem=s4.at[k],
                recv_sem=v4.at[k],
                device_id={"grp": lax.rem(gi + k, ngrp)},
                device_id_type=MESH,
            )
        )
    for copy in sends:
        copy.start()
    hid_out = pltpu.make_async_copy(qs_ref, hid_hbm, store_sem.at[0])
    hid_out.start()
    for copy in sends:
        copy.wait()
    total = ss_ref[...]
    for k in range(1, ngrp):
        total = total + rs_ref[k]
    inverse = lax.rsqrt(total * (1.0 / D) + 1e-06)
    inv_ref[...] = inverse[0:1, :]
    inv_out = pltpu.make_async_copy(inv_ref, inv_hbm, store_sem.at[1])
    inv_out.start()

    @pl.when(me < nctx - 1)
    def _():
        halo.wait_send()

    for k in range(1, BACK + 1):

        @pl.when(z + k < zn)
        def _(k=k):
            totals[k - 1].wait_send()

    hid_out.wait()
    inv_out.wait()


def shards(
    nctx,
    ngrp,
    query_in,
    key_in,
    value_in,
    short_taps,
    decay_rate,
    residues,
    doc_lengths,
    residual,
    norm_gain,
):
    tok, chans = query_in.shape
    modes = decay_rate.shape[0]
    tiles = chans // 128
    quarter = modes // YN
    anywhere = pl.BlockSpec(memory_space=pl.ANY)
    state = (modes, tiles, 128)
    part = (quarter, tiles, 128)
    chunked = (tok // 8, tiles * 8, 128)
    dma = pltpu.SemaphoreType.DMA
    hidden, inverse = pl.pallas_call(
        functools.partial(block_kernel, nctx, ngrp),
        out_shape=(
            jax.ShapeDtypeStruct((tok, chans), F32),
            jax.ShapeDtypeStruct((1, tok), F32),
        ),
        in_specs=[anywhere] * 8,
        out_specs=(anywhere, anywhere),
        scratch_shapes=[
            pltpu.SMEM(doc_lengths.shape, jnp.int32),
            pltpu.VMEM((tok, chans), BF16),
            pltpu.VMEM((tok, chans), BF16),
            pltpu.VMEM((tok, chans), BF16),
            pltpu.VMEM(short_taps.shape, F32),
            pltpu.VMEM(decay_rate.shape, F32),
            pltpu.VMEM(residues.shape, F32),
            pltpu.VMEM((tok, chans), BF16),
            pltpu.VMEM((1, tok), F32),
            pltpu.VMEM((8, chans), F32),
            pltpu.VMEM((8, chans), F32),
            pltpu.VMEM((8, chans), BF16),
            pltpu.VMEM((8, chans), BF16),
            pltpu.VMEM((tok, chans), F32),
            pltpu.VMEM(chunked, F32),
            pltpu.VMEM(chunked, F32),
            pltpu.VMEM((tok, 128), F32),
            pltpu.VMEM((tok, 128), F32),
            pltpu.VMEM((tok, 128), F32),
            pltpu.VMEM((nctx, 128), F32),
            pltpu.VMEM((3, tiles * modes, 128), F32),
            pltpu.VMEM(state, F32),
            pltpu.VMEM(state, F32),
            pltpu.VMEM(state, F32),
            pltpu.VMEM(state, F32),
            pltpu.VMEM((YN,) + part, F32),
            pltpu.VMEM(part, F32),
            pltpu.VMEM(part, BF16),
            pltpu.VMEM(part, F32),
            pltpu.VMEM((BACK - 1,) + part, BF16),
            pltpu.VMEM((YN,) + part, F32),
            pltpu.VMEM((YN,) + part, F32),
            pltpu.VMEM((8, 128), F32),
            pltpu.VMEM((ngrp, 8, 128), F32),
            dma((8,)),
            dma((2,)),
            dma,
            dma,
            dma((YN,)),
            dma((YN,)),
            dma((BACK,)),
            dma((BACK,)),
            dma((YN,)),
            dma((YN,)),
            dma((ngrp,)),
            dma((ngrp,)),
            pltpu.SemaphoreType.REGULAR,
        ],
        compiler_params=pltpu.CompilerParams(collective_id=0, has_side_effects=True),
        name="hyena_block",
    )(
        doc_lengths,
        query_in,
        key_in,
        value_in,
        short_taps,
        decay_rate,
        residues,
        residual,
    )
    normed = (hidden * inverse.reshape(tok)[:, None] * norm_gain[None, :]).astype(BF16)
    return (hidden.astype(BF16), normed)


def solution(mesh):
    return jax.shard_map(
        functools.partial(shards, mesh.shape["ctx"], mesh.shape["grp"]),
        mesh=mesh,
        in_specs=(
            P("ctx", "grp"),
            P("ctx", "grp"),
            P("ctx", "grp"),
            P(None, None, "grp"),
            P(None, "grp"),
            P(None, "grp"),
            P(),
            P("ctx", "grp"),
            P("grp"),
        ),
        out_specs=(P("ctx", "grp"), P("ctx", "grp")),
        check_vma=False,
    )
```

```python
import functools

import jax
import jax.numpy as jnp
from jax import lax
from jax.experimental import pallas as pl
from jax.experimental.pallas import tpu as pltpu
from jax.sharding import PartitionSpec as P

D = 8192
MESH = pl.DeviceIdType.MESH
F32 = jnp.float32
BF16 = jnp.bfloat16
YN = 4
BACK = 4


def decay_weight(rate, residue):
    x = 2.0 * rate
    series = 1.0 - x / 8.0
    for k in (7.0, 6.0, 5.0, 4.0, 3.0, 2.0):
        series = 1.0 - (x / k) * series
    one_minus = jnp.where(x < 0.25, x * series, 1.0 - jnp.exp(-x))
    return residue * jnp.sqrt(one_minus)


def block_kernel(
    nctx,
    ngrp,
    doc_hbm,
    q_hbm,
    k_hbm,
    v_hbm,
    taps_hbm,
    rate_hbm,
    res_hbm,
    resid_hbm,
    gain_hbm,
    out_hbm,
    doc_ref,
    q_ref,
    k_ref,
    v_ref,
    taps_ref,
    rate_ref,
    res_ref,
    resid_ref,
    gain_ref,
    out_ref,
    tail_ref,
    halo_ref,
    tail16_ref,
    halo16_ref,
    qs_ref,
    g_ref,
    y_ref,
    keep_ref,
    pre_ref,
    late_ref,
    carry_ref,
    nat_ref,
    a_ref,
    w_ref,
    rate3_ref,
    e_ref,
    r1_ref,
    t_ref,
    t16_ref,
    r2_ref,
    r216_ref,
    i_ref,
    r3_ref,
    ss_ref,
    rs_ref,
    load_sem,
    store_sem,
    halo_send,
    halo_recv,
    s1,
    v1,
    s2,
    v2,
    s3,
    v3,
    s4,
    v4,
    ready,
):
    tok, chans = q_ref.shape
    lanes = 128
    sub = 8
    chunks = tok // sub
    tiles = chans // lanes
    modes = rate_ref.shape[0]
    ndoc = doc_ref.shape[0]
    quarter = modes // YN
    zn = nctx // YN
    me = lax.axis_index("ctx")
    gi = lax.axis_index("grp")
    z = me // YN
    yy = lax.rem(me, YN)

    def in_plane(k):
        return z * YN + lax.rem(yy + k, YN)

    def plane(k):
        return (z + k) * YN + yy

    barrier = pltpu.get_barrier_semaphore()
    @pl.when(me > 0)
    def _():
        pl.semaphore_signal(barrier, inc=1, device_id={"ctx": me - 1}, device_id_type=MESH)

    for k in range(1, YN):
        pl.semaphore_signal(
            barrier, inc=1, device_id={"ctx": in_plane(YN - k)}, device_id_type=MESH
        )
    for k in range(1, BACK + 1):

        @pl.when(z + k < zn)
        def _(k=k):
            pl.semaphore_signal(barrier, inc=1, device_id={"ctx": plane(k)}, device_id_type=MESH)

    for k in range(1, ngrp):
        pl.semaphore_signal(
            barrier, inc=1, device_id={"grp": lax.rem(gi + ngrp - k, ngrp)}, device_id_type=MESH
        )

    pairs = (
        (doc_hbm, doc_ref),
        (k_hbm, k_ref),
        (v_hbm, v_ref),
        (q_hbm, q_ref),
        (rate_hbm, rate_ref),
        (taps_hbm, taps_ref),
        (res_hbm, res_ref),
        (resid_hbm, resid_ref),
        (gain_hbm, gain_ref),
    )
    loads = [
        pltpu.make_async_copy(src, dst, load_sem.at[i]) for i, (src, dst) in enumerate(pairs)
    ]
    for copy in loads:
        copy.start()

    loads[0].wait()
    row = lax.broadcasted_iota(jnp.int32, (tok, lanes), 0)
    p0 = me * tok
    start = jnp.int32(0)
    first = jnp.int32(tok)
    last = jnp.int32(-1)
    before = jnp.int32(0)
    fresh = jnp.zeros((tok, lanes), F32)
    for d in range(ndoc):
        rel = start - p0
        fresh = jnp.where(row == rel, 1.0, fresh)
        before = jnp.where(rel == -1, 1, before)
        first = jnp.where(rel >= 0, jnp.minimum(first, rel), first)
        last = jnp.where((rel >= 0) & (rel < tok), rel, last)
        start = start + doc_ref[d]
    keep_one = 1.0 - fresh
    keep_ref[...] = keep_one
    keep_prev = jnp.where(row == 0, (1 - before).astype(F32), pltpu.roll(keep_one, 1, 0))
    keep_two = keep_one * keep_prev
    pre_ref[...] = jnp.where(row < first, 1.0, 0.0)
    late_ref[...] = jnp.where(row >= last, 1.0, 0.0)

    for copy in loads[1:4]:
        copy.wait()
    for i, ref in enumerate((q_ref, k_ref, v_ref)):
        tail_ref[2 * i : 2 * i + 2, :] = ref[tok - 16 :, :].astype(F32)[14:16]
    tail_ref[6:8, :] = jnp.zeros((2, chans), F32)
    tail16_ref[...] = tail_ref[...].astype(BF16)
    for copy in loads[4:]:
        copy.wait()

    def by_mode(slot, value, dest):
        for j in range(tiles):
            nat_ref[slot, j * modes : (j + 1) * modes, :] = value[:, j * lanes : (j + 1) * lanes]
        for n in range(modes):
            dest[n] = nat_ref[slot, pl.ds(n, tiles, stride=modes), :]

    rate = rate_ref[...]
    by_mode(0, jnp.exp(-rate), a_ref)
    by_mode(2, rate, rate3_ref)

    def short(ref, i, j, rows, rim):
        cols = slice(j * lanes, (j + 1) * lanes)
        x = (ref[:, cols] if rows == tok else ref[0:16, cols]).astype(F32)[0:rows]
        one = pltpu.roll(x, 1, 0)
        two = pltpu.roll(x, 2, 0)
        if rim:
            at = row[0:rows]
            h0 = halo_ref[2 * i : 2 * i + 1, cols]
            h1 = halo_ref[2 * i + 1 : 2 * i + 2, cols]
            one = jnp.where(at == 0, h1, one)
            two = jnp.where(at == 0, h0, jnp.where(at == 1, h1, two))
        return (
            taps_ref[i, 0:1, cols] * x
            + taps_ref[i, 1:2, cols] * (one * keep_one[0:rows])
            + taps_ref[i, 2:3, cols] * (two * keep_two[0:rows])
        )

    for j in range(tiles):
        gate = short(k_ref, 1, j, tok, False) * short(v_ref, 2, j, tok, False)
        gate = gate.astype(BF16).astype(F32).reshape(chunks, sub, lanes)
        g_ref[:, j * sub : (j + 1) * sub, :] = gate

    def gate_at(c, r):
        return g_ref[c, pl.ds(r, tiles, stride=sub), :]

    def late_gate(c, r):
        return gate_at(c, r) * late_ref[pl.ds(c * sub + r, 1), :]

    greeted = (YN - 1) + (ngrp - 1) + jnp.minimum(z, BACK) + jnp.minimum(nctx - 1 - me, 1)
    pl.semaphore_wait(barrier, greeted)
    halo = pltpu.make_async_remote_copy(
        src_ref=tail16_ref,
        dst_ref=halo16_ref,
        send_sem=halo_send,
        recv_sem=halo_recv,
        device_id={"ctx": me + 1},
        device_id_type=MESH,
    )

    @pl.when(me < nctx - 1)
    def _():
        halo.start()

    @pl.when(me == 0)
    def _():
        halo16_ref[...] = jnp.zeros(halo16_ref.shape, BF16)

    for k in range(1, BACK + 1):

        @pl.when(z >= k)
        def _(k=k):
            pl.semaphore_signal(ready, inc=1, device_id={"ctx": plane(-k)}, device_id_type=MESH)

    def end_chunk(c, states, first_row=0):
        for r in range(first_row, sub):
            g = late_gate(c, r)
            states = tuple(a_ref[n] * states[n] + g for n in range(modes))
        return states

    zero = jnp.zeros((tiles, lanes), F32)
    states = end_chunk(0, (zero,) * modes, 2)
    states = lax.fori_loop(1, chunks, end_chunk, states)
    for n in range(modes):
        e_ref[n] = states[n]

    by_mode(1, decay_weight(rate, res_ref[...]), w_ref)
    brow = lax.broadcasted_iota(jnp.int32, (nctx, lanes), 0)
    opens = jnp.zeros((nctx, lanes), F32)
    start = jnp.int32(0)
    for d in range(ndoc):
        opens = jnp.where(brow == start // tok, 1.0, opens)
        start = start + doc_ref[d]
    carry_ref[...] = 1.0 - opens
    @pl.when(me > 0)
    def _():
        halo.wait_recv()

    halo_ref[...] = halo16_ref[...].astype(F32)
    for j in range(tiles):
        gate = short(k_ref, 1, j, sub, True) * short(v_ref, 2, j, sub, True)
        g_ref[0, j * sub : (j + 1) * sub, :] = gate.astype(BF16).astype(F32)
    g0 = late_gate(0, 0)
    g1 = late_gate(0, 1)
    for n in range(modes):
        e_ref[n] = e_ref[n] + jnp.exp(-float(tok - 2) * rate3_ref[n]) * (g1 + a_ref[n] * g0)

    sends = []
    for k in range(1, YN):
        to = lax.rem(yy + k, YN)
        sends.append(
            pltpu.make_async_remote_copy(
                src_ref=e_ref.at[pl.ds(to * quarter, quarter)],
                dst_ref=r1_ref.at[k],
                send_sem=s1.at[k],
                recv_sem=v1.at[k],
                device_id={"ctx": in_plane(k)},
                device_id_type=MESH,
            )
        )
    for copy in sends:
        copy.start()
    r1_ref[0] = e_ref[pl.ds(yy * quarter, quarter)]
    rate_q = rate3_ref[pl.ds(yy * quarter, quarter)]
    decay_blk = jnp.exp(-float(tok) * rate_q)
    decay_plane = jnp.exp(-float(tok * YN) * rate_q)

    def carry_of(block):
        return carry_ref[pl.ds(block, 1), :][None]

    def plane_carry(k):
        base = lax.rem(z - k + zn, zn) * YN
        value = carry_of(base)
        for j in range(1, YN):
            value = value * carry_of(base + j)
        return value

    def scan_chunk(c, states):
        for r in range(sub):
            g = gate_at(c, r)
            keep = keep_ref[pl.ds(c * sub + r, 1), :]
            new = []
            total = None
            for n in range(modes):
                s = a_ref[n] * (keep * states[n]) + g
                term = w_ref[n] * s
                total = term if total is None else total + term
                new.append(s)
            y_ref[c, pl.ds(r, tiles, stride=sub), :] = total
            states = tuple(new)
        return states

    states = lax.fori_loop(0, chunks // 2, scan_chunk, (zero,) * modes)

    for copy in sends:
        copy.wait()

    ends = [r1_ref[lax.rem(yy - j + YN, YN)] for j in range(YN)]
    total = ends[0]
    for j in range(1, YN):
        total = ends[j] + decay_blk * carry_of(z * YN + j) * total
    t_ref[...] = total
    t16_ref[...] = total.astype(BF16)

    sends = []
    for k in range(1, BACK + 1):
        sends.append(
            pltpu.make_async_remote_copy(
                src_ref=t_ref if k == 1 else t16_ref,
                dst_ref=r2_ref if k == 1 else r216_ref.at[k - 2],
                send_sem=s2.at[k - 1],
                recv_sem=v2.at[k - 1],
                device_id={"ctx": plane(k)},
                device_id_type=MESH,
            )
        )
    totals = sends
    @pl.when(z < zn - 1)
    def _():
        pl.semaphore_wait(ready, jnp.minimum(zn - 1 - z, BACK))

    for k in range(BACK, 0, -1):

        @pl.when(z + k < zn)
        def _(k=k):
            totals[k - 1].start()

        @pl.when(z < k)
        def _(k=k):
            if k == 1:
                r2_ref[...] = jnp.zeros(t_ref.shape, F32)
            else:
                r216_ref[k - 2] = jnp.zeros(t_ref.shape, BF16)

    states = lax.fori_loop(chunks // 2, 3 * chunks // 4, scan_chunk, states)
    for j in range(tiles):
        cols = slice(j * lanes, (j + 1) * lanes)
        qs_ref[:, cols] = short(q_ref, 0, j, tok, True)
    for k in range(1, BACK + 1):

        @pl.when(z >= k)
        def _(k=k):
            totals[k - 1].wait_recv()

    enter = r216_ref[BACK - 2].astype(F32)
    for k in range(BACK - 1, 0, -1):
        mine = r2_ref[...] if k == 1 else r216_ref[k - 2].astype(F32)
        enter = mine + decay_plane * plane_carry(k) * enter
    for j in range(YN):
        i_ref[j] = enter
        if j < YN - 1:
            enter = ends[j] + decay_blk * carry_of(z * YN + j) * enter

    sends = []
    for k in range(1, YN):
        to = lax.rem(yy + k, YN)
        sends.append(
            pltpu.make_async_remote_copy(
                src_ref=i_ref.at[to],
                dst_ref=r3_ref.at[k],
                send_sem=s3.at[k],
                recv_sem=v3.at[k],
                device_id={"ctx": in_plane(k)},
                device_id_type=MESH,
            )
        )
    for copy in sends:
        copy.start()
    r3_ref[0] = i_ref[yy]
    lax.fori_loop(3 * chunks // 4, chunks, scan_chunk, states)
    for copy in sends:
        copy.wait()

    entering = []
    for m in range(YN):
        part = r3_ref[lax.rem(yy - m + YN, YN)]
        for n in range(quarter):
            entering.append(w_ref[m * quarter + n] * part[n])

    def fix_chunk(c, states):
        for r in range(sub):
            states = tuple(a_ref[n] * states[n] for n in range(modes))
            total = states[0]
            for n in range(1, modes):
                total = total + states[n]
            at = pl.ds(r, tiles, stride=sub)
            y_ref[c, at, :] = y_ref[c, at, :] + pre_ref[pl.ds(c * sub + r, 1), :] * total
        return states

    lax.fori_loop(0, chunks, fix_chunk, tuple(entering))

    squares = jnp.zeros((tok, lanes), F32)
    for j in range(tiles):
        cols = slice(j * lanes, (j + 1) * lanes)
        conv = y_ref[:, j * sub : (j + 1) * sub, :].reshape(tok, lanes)
        conv = conv.astype(BF16).astype(F32)
        hidden = resid_ref[:, cols].astype(F32) + qs_ref[:, cols] * conv
        squares = squares + hidden * hidden
        qs_ref[:, cols] = hidden
    by_token = jnp.sum(squares.T, axis=0, keepdims=True)
    ss_ref[...] = jnp.broadcast_to(by_token, (8, lanes))
    sends = []
    for k in range(1, ngrp):
        sends.append(
            pltpu.make_async_remote_copy(
                src_ref=ss_ref,
                dst_ref=rs_ref.at[k],
                send_sem=s4.at[k],
                recv_sem=v4.at[k],
                device_id={"grp": lax.rem(gi + k, ngrp)},
                device_id_type=MESH,
            )
        )
    for copy in sends:
        copy.start()
    out_ref[0] = qs_ref[...].astype(BF16)
    hid_out = pltpu.make_async_copy(out_ref.at[0], out_hbm.at[0], store_sem.at[0])
    hid_out.start()
    for copy in sends:
        copy.wait()
    total = ss_ref[...]
    for k in range(1, ngrp):
        total = total + rs_ref[k]
    inverse = lax.rsqrt(total * (1.0 / D) + 1e-06)
    inverse = jnp.broadcast_to(inverse[0:1, :], (lanes, tok)).T
    for j in range(tiles):
        cols = slice(j * lanes, (j + 1) * lanes)
        out_ref[1, :, cols] = (qs_ref[:, cols] * inverse * gain_ref[:, cols]).astype(BF16)
    norm_out = pltpu.make_async_copy(out_ref.at[1], out_hbm.at[1], store_sem.at[1])
    norm_out.start()

    @pl.when(me < nctx - 1)
    def _():
        halo.wait_send()

    for k in range(1, BACK + 1):

        @pl.when(z + k < zn)
        def _(k=k):
            totals[k - 1].wait_send()

    hid_out.wait()
    norm_out.wait()


def shards(
    nctx,
    ngrp,
    query_in,
    key_in,
    value_in,
    short_taps,
    decay_rate,
    residues,
    doc_lengths,
    residual,
    norm_gain,
):
    tok, chans = query_in.shape
    modes = decay_rate.shape[0]
    tiles = chans // 128
    quarter = modes // YN
    anywhere = pl.BlockSpec(memory_space=pl.ANY)
    state = (modes, tiles, 128)
    part = (quarter, tiles, 128)
    chunked = (tok // 8, tiles * 8, 128)
    dma = pltpu.SemaphoreType.DMA
    both = pl.pallas_call(
        functools.partial(block_kernel, nctx, ngrp),
        out_shape=jax.ShapeDtypeStruct((2, tok, chans), BF16),
        in_specs=[anywhere] * 9,
        out_specs=anywhere,
        scratch_shapes=[
            pltpu.SMEM(doc_lengths.shape, jnp.int32),
            pltpu.VMEM((tok, chans), BF16),
            pltpu.VMEM((tok, chans), BF16),
            pltpu.VMEM((tok, chans), BF16),
            pltpu.VMEM(short_taps.shape, F32),
            pltpu.VMEM(decay_rate.shape, F32),
            pltpu.VMEM(residues.shape, F32),
            pltpu.VMEM((tok, chans), BF16),
            pltpu.VMEM((1, chans), F32),
            pltpu.VMEM((2, tok, chans), BF16),
            pltpu.VMEM((8, chans), F32),
            pltpu.VMEM((8, chans), F32),
            pltpu.VMEM((8, chans), BF16),
            pltpu.VMEM((8, chans), BF16),
            pltpu.VMEM((tok, chans), F32),
            pltpu.VMEM(chunked, F32),
            pltpu.VMEM(chunked, F32),
            pltpu.VMEM((tok, 128), F32),
            pltpu.VMEM((tok, 128), F32),
            pltpu.VMEM((tok, 128), F32),
            pltpu.VMEM((nctx, 128), F32),
            pltpu.VMEM((3, tiles * modes, 128), F32),
            pltpu.VMEM(state, F32),
            pltpu.VMEM(state, F32),
            pltpu.VMEM(state, F32),
            pltpu.VMEM(state, F32),
            pltpu.VMEM((YN,) + part, F32),
            pltpu.VMEM(part, F32),
            pltpu.VMEM(part, BF16),
            pltpu.VMEM(part, F32),
            pltpu.VMEM((BACK - 1,) + part, BF16),
            pltpu.VMEM((YN,) + part, F32),
            pltpu.VMEM((YN,) + part, F32),
            pltpu.VMEM((8, 128), F32),
            pltpu.VMEM((ngrp, 8, 128), F32),
            dma((9,)),
            dma((2,)),
            dma,
            dma,
            dma((YN,)),
            dma((YN,)),
            dma((BACK,)),
            dma((BACK,)),
            dma((YN,)),
            dma((YN,)),
            dma((ngrp,)),
            dma((ngrp,)),
            pltpu.SemaphoreType.REGULAR,
        ],
        compiler_params=pltpu.CompilerParams(collective_id=0, has_side_effects=True),
        name="hyena_block",
    )(
        doc_lengths,
        query_in,
        key_in,
        value_in,
        short_taps,
        decay_rate,
        residues,
        residual,
        norm_gain.reshape(1, chans),
    )
    return (both[0], both[1])


def solution(mesh):
    return jax.shard_map(
        functools.partial(shards, mesh.shape["ctx"], mesh.shape["grp"]),
        mesh=mesh,
        in_specs=(
            P("ctx", "grp"),
            P("ctx", "grp"),
            P("ctx", "grp"),
            P(None, None, "grp"),
            P(None, "grp"),
            P(None, "grp"),
            P(),
            P("ctx", "grp"),
            P("grp"),
        ),
        out_specs=(P("ctx", "grp"), P("ctx", "grp")),
        check_vma=False,
    )
```

```python
import functools

import jax
import jax.numpy as jnp
from jax import lax
from jax.experimental import pallas as pl
from jax.experimental.pallas import tpu as pltpu
from jax.sharding import PartitionSpec as P

D = 8192
MESH = pl.DeviceIdType.MESH
F32 = jnp.float32
BF16 = jnp.bfloat16
YN = 4
BACK = 4


def decay_weight(rate, residue):
    x = 2.0 * rate
    series = 1.0 - x / 8.0
    for k in (7.0, 6.0, 5.0, 4.0, 3.0, 2.0):
        series = 1.0 - (x / k) * series
    one_minus = jnp.where(x < 0.25, x * series, 1.0 - jnp.exp(-x))
    return residue * jnp.sqrt(one_minus)


def block_kernel(
    nctx,
    ngrp,
    doc_hbm,
    q_hbm,
    k_hbm,
    v_hbm,
    taps_hbm,
    rate_hbm,
    res_hbm,
    resid_hbm,
    gain_hbm,
    out_hbm,
    doc_ref,
    q_ref,
    k_ref,
    v_ref,
    taps_ref,
    rate_ref,
    res_ref,
    resid_ref,
    gain_ref,
    out_ref,
    tail_ref,
    halo_ref,
    tail16_ref,
    halo16_ref,
    qs_ref,
    g_ref,
    y_ref,
    keep_ref,
    pre_ref,
    late_ref,
    carry_ref,
    nat_ref,
    a_ref,
    w_ref,
    rate3_ref,
    e_ref,
    r1_ref,
    t_ref,
    t16_ref,
    r2_ref,
    r216_ref,
    i_ref,
    r3_ref,
    ss_ref,
    rs_ref,
    load_sem,
    store_sem,
    halo_send,
    halo_recv,
    s1,
    v1,
    s2,
    v2,
    s3,
    v3,
    s4,
    v4,
    ready,
):
    tok, chans = q_ref.shape
    lanes = 128
    sub = 8
    chunks = tok // sub
    tiles = chans // lanes
    modes = rate_ref.shape[0]
    ndoc = doc_ref.shape[0]
    quarter = modes // YN
    zn = nctx // YN
    me = lax.axis_index("ctx")
    gi = lax.axis_index("grp")
    z = me // YN
    yy = lax.rem(me, YN)

    def in_plane(k):
        return z * YN + lax.rem(yy + k, YN)

    def plane(k):
        return (z + k) * YN + yy

    barrier = pltpu.get_barrier_semaphore()
    @pl.when(me > 0)
    def _():
        pl.semaphore_signal(barrier, inc=1, device_id={"ctx": me - 1}, device_id_type=MESH)

    for k in range(1, YN):
        pl.semaphore_signal(
            barrier, inc=1, device_id={"ctx": in_plane(YN - k)}, device_id_type=MESH
        )
    for k in range(1, BACK + 1):

        @pl.when(z + k < zn)
        def _(k=k):
            pl.semaphore_signal(barrier, inc=1, device_id={"ctx": plane(k)}, device_id_type=MESH)

    for k in range(1, ngrp):
        pl.semaphore_signal(
            barrier, inc=1, device_id={"grp": lax.rem(gi + ngrp - k, ngrp)}, device_id_type=MESH
        )

    pairs = (
        (doc_hbm, doc_ref),
        (k_hbm, k_ref),
        (v_hbm, v_ref),
        (q_hbm, q_ref),
        (rate_hbm, rate_ref),
        (taps_hbm, taps_ref),
        (res_hbm, res_ref),
        (resid_hbm, resid_ref),
        (gain_hbm, gain_ref),
    )
    loads = [
        pltpu.make_async_copy(src, dst, load_sem.at[i]) for i, (src, dst) in enumerate(pairs)
    ]
    for copy in loads:
        copy.start()

    loads[0].wait()
    row = lax.broadcasted_iota(jnp.int32, (tok, lanes), 0)
    p0 = me * tok
    start = jnp.int32(0)
    first = jnp.int32(tok)
    last = jnp.int32(-1)
    before = jnp.int32(0)
    fresh = jnp.zeros((tok, lanes), F32)
    for d in range(ndoc):
        rel = start - p0
        fresh = jnp.where(row == rel, 1.0, fresh)
        before = jnp.where(rel == -1, 1, before)
        first = jnp.where(rel >= 0, jnp.minimum(first, rel), first)
        last = jnp.where((rel >= 0) & (rel < tok), rel, last)
        start = start + doc_ref[d]
    keep_one = 1.0 - fresh
    keep_ref[...] = keep_one
    keep_prev = jnp.where(row == 0, (1 - before).astype(F32), pltpu.roll(keep_one, 1, 0))
    keep_two = keep_one * keep_prev
    pre_ref[...] = jnp.where(row < first, 1.0, 0.0)
    late_ref[...] = jnp.where(row >= last, 1.0, 0.0)

    for copy in loads[1:4]:
        copy.wait()
    for i, ref in enumerate((q_ref, k_ref, v_ref)):
        tail_ref[2 * i : 2 * i + 2, :] = ref[tok - 16 :, :].astype(F32)[14:16]
    tail_ref[6:8, :] = jnp.zeros((2, chans), F32)
    tail16_ref[...] = tail_ref[...].astype(BF16)
    for copy in loads[4:]:
        copy.wait()

    def by_mode(slot, value, dest):
        for j in range(tiles):
            nat_ref[slot, j * modes : (j + 1) * modes, :] = value[:, j * lanes : (j + 1) * lanes]
        for n in range(modes):
            dest[n] = nat_ref[slot, pl.ds(n, tiles, stride=modes), :]

    rate = rate_ref[...]
    by_mode(0, jnp.exp(-rate), a_ref)
    by_mode(2, rate, rate3_ref)

    def short(ref, i, j, rows, rim):
        cols = slice(j * lanes, (j + 1) * lanes)
        x = (ref[:, cols] if rows == tok else ref[0:16, cols]).astype(F32)[0:rows]
        one = pltpu.roll(x, 1, 0)
        two = pltpu.roll(x, 2, 0)
        if rim:
            at = row[0:rows]
            h0 = halo_ref[2 * i : 2 * i + 1, cols]
            h1 = halo_ref[2 * i + 1 : 2 * i + 2, cols]
            one = jnp.where(at == 0, h1, one)
            two = jnp.where(at == 0, h0, jnp.where(at == 1, h1, two))
        return (
            taps_ref[i, 0:1, cols] * x
            + taps_ref[i, 1:2, cols] * (one * keep_one[0:rows])
            + taps_ref[i, 2:3, cols] * (two * keep_two[0:rows])
        )

    greeted = (YN - 1) + (ngrp - 1) + jnp.minimum(z, BACK) + jnp.minimum(nctx - 1 - me, 1)
    pl.semaphore_wait(barrier, greeted)
    halo = pltpu.make_async_remote_copy(
        src_ref=tail16_ref,
        dst_ref=halo16_ref,
        send_sem=halo_send,
        recv_sem=halo_recv,
        device_id={"ctx": me + 1},
        device_id_type=MESH,
    )

    @pl.when(me < nctx - 1)
    def _():
        halo.start()

    @pl.when(me == 0)
    def _():
        halo16_ref[...] = jnp.zeros(halo16_ref.shape, BF16)

    for k in range(1, BACK + 1):

        @pl.when(z >= k)
        def _(k=k):
            pl.semaphore_signal(ready, inc=1, device_id={"ctx": plane(-k)}, device_id_type=MESH)

    for j in range(tiles):
        gate = short(k_ref, 1, j, tok, False) * short(v_ref, 2, j, tok, False)
        gate = gate.astype(BF16).astype(F32).reshape(chunks, sub, lanes)
        g_ref[:, j * sub : (j + 1) * sub, :] = gate

    def gate_at(c, r):
        return g_ref[c, pl.ds(r, tiles, stride=sub), :]

    def late_gate(c, r):
        return gate_at(c, r) * late_ref[pl.ds(c * sub + r, 1), :]

    def end_chunk(c, states, first_row=0):
        for r in range(first_row, sub):
            g = late_gate(c, r)
            states = tuple(a_ref[n] * states[n] + g for n in range(modes))
        return states

    zero = jnp.zeros((tiles, lanes), F32)
    states = end_chunk(0, (zero,) * modes, 2)
    states = lax.fori_loop(1, chunks, end_chunk, states)
    for n in range(modes):
        e_ref[n] = states[n]

    by_mode(1, decay_weight(rate, res_ref[...]), w_ref)
    brow = lax.broadcasted_iota(jnp.int32, (nctx, lanes), 0)
    opens = jnp.zeros((nctx, lanes), F32)
    start = jnp.int32(0)
    for d in range(ndoc):
        opens = jnp.where(brow == start // tok, 1.0, opens)
        start = start + doc_ref[d]
    carry_ref[...] = 1.0 - opens
    @pl.when(me > 0)
    def _():
        halo.wait_recv()

    halo_ref[...] = halo16_ref[...].astype(F32)
    for j in range(tiles):
        gate = short(k_ref, 1, j, sub, True) * short(v_ref, 2, j, sub, True)
        g_ref[0, j * sub : (j + 1) * sub, :] = gate.astype(BF16).astype(F32)
    g0 = late_gate(0, 0)
    g1 = late_gate(0, 1)
    for n in range(modes):
        e_ref[n] = e_ref[n] + jnp.exp(-float(tok - 2) * rate3_ref[n]) * (g1 + a_ref[n] * g0)

    sends = []
    for k in range(1, YN):
        to = lax.rem(yy + k, YN)
        sends.append(
            pltpu.make_async_remote_copy(
                src_ref=e_ref.at[pl.ds(to * quarter, quarter)],
                dst_ref=r1_ref.at[k],
                send_sem=s1.at[k],
                recv_sem=v1.at[k],
                device_id={"ctx": in_plane(k)},
                device_id_type=MESH,
            )
        )
    for copy in sends:
        copy.start()
    r1_ref[0] = e_ref[pl.ds(yy * quarter, quarter)]
    rate_q = rate3_ref[pl.ds(yy * quarter, quarter)]
    decay_blk = jnp.exp(-float(tok) * rate_q)
    decay_plane = jnp.exp(-float(tok * YN) * rate_q)

    def carry_of(block):
        return carry_ref[pl.ds(block, 1), :][None]

    def plane_carry(k):
        base = lax.rem(z - k + zn, zn) * YN
        value = carry_of(base)
        for j in range(1, YN):
            value = value * carry_of(base + j)
        return value

    def scan_chunk(c, states):
        for r in range(sub):
            g = gate_at(c, r)
            keep = keep_ref[pl.ds(c * sub + r, 1), :]
            new = []
            total = None
            for n in range(modes):
                s = a_ref[n] * (keep * states[n]) + g
                term = w_ref[n] * s
                total = term if total is None else total + term
                new.append(s)
            y_ref[c, pl.ds(r, tiles, stride=sub), :] = total
            states = tuple(new)
        return states

    states = lax.fori_loop(0, chunks // 2, scan_chunk, (zero,) * modes)

    for copy in sends:
        copy.wait()

    ends = [r1_ref[lax.rem(yy - j + YN, YN)] for j in range(YN)]
    total = ends[0]
    for j in range(1, YN):
        total = ends[j] + decay_blk * carry_of(z * YN + j) * total
    t_ref[...] = total
    t16_ref[...] = total.astype(BF16)

    sends = []
    for k in range(1, BACK + 1):
        sends.append(
            pltpu.make_async_remote_copy(
                src_ref=t_ref if k == 1 else t16_ref,
                dst_ref=r2_ref if k == 1 else r216_ref.at[k - 2],
                send_sem=s2.at[k - 1],
                recv_sem=v2.at[k - 1],
                device_id={"ctx": plane(k)},
                device_id_type=MESH,
            )
        )
    totals = sends
    @pl.when(z < zn - 1)
    def _():
        pl.semaphore_wait(ready, jnp.minimum(zn - 1 - z, BACK))

    for k in range(BACK, 0, -1):

        @pl.when(z + k < zn)
        def _(k=k):
            totals[k - 1].start()

        @pl.when(z < k)
        def _(k=k):
            if k == 1:
                r2_ref[...] = jnp.zeros(t_ref.shape, F32)
            else:
                r216_ref[k - 2] = jnp.zeros(t_ref.shape, BF16)

    states = lax.fori_loop(chunks // 2, 3 * chunks // 4, scan_chunk, states)
    for j in range(tiles):
        cols = slice(j * lanes, (j + 1) * lanes)
        qs_ref[:, cols] = short(q_ref, 0, j, tok, True)
    for k in range(1, BACK + 1):

        @pl.when(z >= k)
        def _(k=k):
            totals[k - 1].wait_recv()

    enter = r216_ref[BACK - 2].astype(F32)
    for k in range(BACK - 1, 0, -1):
        mine = r2_ref[...] if k == 1 else r216_ref[k - 2].astype(F32)
        enter = mine + decay_plane * plane_carry(k) * enter
    for j in range(YN):
        i_ref[j] = enter
        if j < YN - 1:
            enter = ends[j] + decay_blk * carry_of(z * YN + j) * enter

    sends = []
    for k in range(1, YN):
        to = lax.rem(yy + k, YN)
        sends.append(
            pltpu.make_async_remote_copy(
                src_ref=i_ref.at[to],
                dst_ref=r3_ref.at[k],
                send_sem=s3.at[k],
                recv_sem=v3.at[k],
                device_id={"ctx": in_plane(k)},
                device_id_type=MESH,
            )
        )
    for copy in sends:
        copy.start()
    r3_ref[0] = i_ref[yy]
    lax.fori_loop(3 * chunks // 4, chunks, scan_chunk, states)
    for copy in sends:
        copy.wait()

    entering = []
    for m in range(YN):
        part = r3_ref[lax.rem(yy - m + YN, YN)]
        for n in range(quarter):
            entering.append(w_ref[m * quarter + n] * part[n])

    def fix_chunk(c, states):
        for r in range(sub):
            states = tuple(a_ref[n] * states[n] for n in range(modes))
            total = states[0]
            for n in range(1, modes):
                total = total + states[n]
            at = pl.ds(r, tiles, stride=sub)
            y_ref[c, at, :] = y_ref[c, at, :] + pre_ref[pl.ds(c * sub + r, 1), :] * total
        return states

    lax.fori_loop(0, chunks, fix_chunk, tuple(entering))

    squares = jnp.zeros((tok, lanes), F32)
    for j in range(tiles):
        cols = slice(j * lanes, (j + 1) * lanes)
        conv = y_ref[:, j * sub : (j + 1) * sub, :].reshape(tok, lanes)
        conv = conv.astype(BF16).astype(F32)
        hidden = resid_ref[:, cols].astype(F32) + qs_ref[:, cols] * conv
        squares = squares + hidden * hidden
        qs_ref[:, cols] = hidden
    by_token = jnp.sum(squares.T, axis=0, keepdims=True)
    ss_ref[...] = jnp.broadcast_to(by_token, (8, lanes))
    sends = []
    for k in range(1, ngrp):
        sends.append(
            pltpu.make_async_remote_copy(
                src_ref=ss_ref,
                dst_ref=rs_ref.at[k],
                send_sem=s4.at[k],
                recv_sem=v4.at[k],
                device_id={"grp": lax.rem(gi + k, ngrp)},
                device_id_type=MESH,
            )
        )
    for copy in sends:
        copy.start()
    out_ref[0] = qs_ref[...].astype(BF16)
    hid_out = pltpu.make_async_copy(out_ref.at[0], out_hbm.at[0], store_sem.at[0])
    hid_out.start()
    for copy in sends:
        copy.wait()
    total = ss_ref[...]
    for k in range(1, ngrp):
        total = total + rs_ref[k]
    inverse = lax.rsqrt(total * (1.0 / D) + 1e-06)
    inverse = jnp.broadcast_to(inverse[0:1, :], (lanes, tok)).T
    for j in range(tiles):
        cols = slice(j * lanes, (j + 1) * lanes)
        out_ref[1, :, cols] = (qs_ref[:, cols] * inverse * gain_ref[:, cols]).astype(BF16)
    norm_out = pltpu.make_async_copy(out_ref.at[1], out_hbm.at[1], store_sem.at[1])
    norm_out.start()

    @pl.when(me < nctx - 1)
    def _():
        halo.wait_send()

    for k in range(1, BACK + 1):

        @pl.when(z + k < zn)
        def _(k=k):
            totals[k - 1].wait_send()

    hid_out.wait()
    norm_out.wait()


def shards(
    nctx,
    ngrp,
    query_in,
    key_in,
    value_in,
    short_taps,
    decay_rate,
    residues,
    doc_lengths,
    residual,
    norm_gain,
):
    tok, chans = query_in.shape
    modes = decay_rate.shape[0]
    tiles = chans // 128
    quarter = modes // YN
    anywhere = pl.BlockSpec(memory_space=pl.ANY)
    state = (modes, tiles, 128)
    part = (quarter, tiles, 128)
    chunked = (tok // 8, tiles * 8, 128)
    dma = pltpu.SemaphoreType.DMA
    both = pl.pallas_call(
        functools.partial(block_kernel, nctx, ngrp),
        out_shape=jax.ShapeDtypeStruct((2, tok, chans), BF16),
        in_specs=[anywhere] * 9,
        out_specs=anywhere,
        scratch_shapes=[
            pltpu.SMEM(doc_lengths.shape, jnp.int32),
            pltpu.VMEM((tok, chans), BF16),
            pltpu.VMEM((tok, chans), BF16),
            pltpu.VMEM((tok, chans), BF16),
            pltpu.VMEM(short_taps.shape, F32),
            pltpu.VMEM(decay_rate.shape, F32),
            pltpu.VMEM(residues.shape, F32),
            pltpu.VMEM((tok, chans), BF16),
            pltpu.VMEM((1, chans), F32),
            pltpu.VMEM((2, tok, chans), BF16),
            pltpu.VMEM((8, chans), F32),
            pltpu.VMEM((8, chans), F32),
            pltpu.VMEM((8, chans), BF16),
            pltpu.VMEM((8, chans), BF16),
            pltpu.VMEM((tok, chans), F32),
            pltpu.VMEM(chunked, F32),
            pltpu.VMEM(chunked, F32),
            pltpu.VMEM((tok, 128), F32),
            pltpu.VMEM((tok, 128), F32),
            pltpu.VMEM((tok, 128), F32),
            pltpu.VMEM((nctx, 128), F32),
            pltpu.VMEM((3, tiles * modes, 128), F32),
            pltpu.VMEM(state, F32),
            pltpu.VMEM(state, F32),
            pltpu.VMEM(state, F32),
            pltpu.VMEM(state, F32),
            pltpu.VMEM((YN,) + part, F32),
            pltpu.VMEM(part, F32),
            pltpu.VMEM(part, BF16),
            pltpu.VMEM(part, F32),
            pltpu.VMEM((BACK - 1,) + part, BF16),
            pltpu.VMEM((YN,) + part, F32),
            pltpu.VMEM((YN,) + part, F32),
            pltpu.VMEM((8, 128), F32),
            pltpu.VMEM((ngrp, 8, 128), F32),
            dma((9,)),
            dma((2,)),
            dma,
            dma,
            dma((YN,)),
            dma((YN,)),
            dma((BACK,)),
            dma((BACK,)),
            dma((YN,)),
            dma((YN,)),
            dma((ngrp,)),
            dma((ngrp,)),
            pltpu.SemaphoreType.REGULAR,
        ],
        compiler_params=pltpu.CompilerParams(collective_id=0, has_side_effects=True),
        name="hyena_block",
    )(
        doc_lengths,
        query_in,
        key_in,
        value_in,
        short_taps,
        decay_rate,
        residues,
        residual,
        norm_gain.reshape(1, chans),
    )
    return (both[0], both[1])


def solution(mesh):
    return jax.shard_map(
        functools.partial(shards, mesh.shape["ctx"], mesh.shape["grp"]),
        mesh=mesh,
        in_specs=(
            P("ctx", "grp"),
            P("ctx", "grp"),
            P("ctx", "grp"),
            P(None, None, "grp"),
            P(None, "grp"),
            P(None, "grp"),
            P(),
            P("ctx", "grp"),
            P("grp"),
        ),
        out_specs=(P("ctx", "grp"), P("ctx", "grp")),
        check_vma=False,
    )
```
